128 devices in a mesh: gx: 8 (over z, x_hi), yz: 16 (over y, x_lo, core).
Axes of the slice: x: 4 (x_hi: 2, x_lo: 2; x = x_hi * 2 + x_lo), y: 4, z: 4, core: 2. Of those that a mesh axis runs over, the one named last changes fastest.
Arguments:
- features: bfloat16 [65536, 128], P(('gx', 'yz')), may hold values from -6 to 6
- frac: float32 [3, 65536], P(None, ('gx', 'yz')), may hold values from 0 to 1
- neighbours: int32 [32, 65536], P(None, ('gx', 'yz')), may hold values from 0 to 2815
- nbr_mask: int32 [32, 65536], P(None, ('gx', 'yz')), may hold values 0 or 1
- send_list: int32 [32768], P(('gx', 'yz')), may hold values from 0 to 511
- wavevectors: int32 [3, 4096], P(None, ('gx', 'yz')), may hold values from -6 to 6
- w_in: bfloat16 [2, 128, 128], replicated, may hold values from -0.5 to 0.5
- w_filter1: bfloat16 [2, 32, 128], replicated, may hold values from -2 to 2
- w_filter2: bfloat16 [2, 128, 128], replicated, may hold values from -0.5 to 0.5
- w_update1: bfloat16 [2, 128, 128], replicated, may hold values from -0.5 to 0.5
- w_update2: bfloat16 [2, 128, 128], replicated, may hold values from -0.5 to 0.5
- w_charge: bfloat16 [128, 16], replicated, may hold values from -0.5 to 0.5
- screening: float32 [16], replicated, may hold values from 1 to 64
- w_head: bfloat16 [128, 128], replicated, may hold values from -0.5 to 0.5
- w_potential: bfloat16 [16, 128], replicated, may hold values from -1.5 to 1.5
- w_energy: bfloat16 [128], replicated, may hold values from -0.5 to 0.5
Outputs:
- embeddings: bfloat16 [65536, 128], P(('gx', 'yz'))
- potentials: float32 [16, 65536], P(None, ('gx', 'yz'))
- energies: float32 [65536], P(('gx', 'yz'))
The draws below stay inside these ranges and needn't reach their ends.
All inputs are finite; a program needn't handle non-finite values. No bound on the sum of `nbr_mask` on one device may be relied on, other than what follows from the above.
Results may differ from the reference program's by a relative error of at most 0.025.
Values may be sent and summed in bfloat16 or wider, within the bound.
No kernel may reach another device: no remote copies, remote signals or barrier semaphores. Data moves between devices by JAX's collectives and lax.ppermute only.
A program may use at most 64 MiB of HBM per device.

```python
import math
import jax
import jax.numpy as jnp
from jax import lax

C = 128
NR = 32
Q = 16
MODES = 4096
K = 32
LAYERS = 2
HALO_SIDE = 16
ATOMS_DEV = 512
ATOMS = 65536
HALO_DEV = 256
HALO = 32768
N_GX = 8
N_YZ = 16


def touch_ends(values, key, low, largest):
    spot = [jax.random.randint(jax.random.fold_in(key, axis), (), 0, length) for axis, length in enumerate(values.shape)]
    widest = values.shape.index(max(values.shape))
    beside = spot[:widest] + [(spot[widest] + 1) % values.shape[widest]] + spot[widest + 1:]
    return values.at[tuple(spot)].set(low).at[tuple(beside)].set(largest)


def steps_of(rng, dims, shards, smallest, largest):
    def one(position, shards_of):
        steps = jax.random.uniform(jax.random.fold_in(jax.random.fold_in(rng, 6), position), (shards_of,), jnp.float32, smallest / len(shards), largest / len(shards))
        return jnp.repeat(jnp.exp(steps), dims[position] // shards_of).reshape((-1,) + (1,) * (len(dims) - position - 1))

    factor_of = one(*shards[0])
    for cut in shards[1:]:
        factor_of = factor_of * one(*cut)
    return factor_of


def noise(rng, shape, spread, reach, split=(), kind=jnp.bfloat16):
    result = spread * jax.random.normal(rng, shape, jnp.float32)
    if split:
        result = result * steps_of(rng, shape, split, -0.22, 0.18)
    return jnp.clip(result, -reach, reach).astype(kind)


def setup_inputs(seed: int = 0) -> dict:
    key_of = jax.random.split(jax.random.key(seed), 17)
    features = noise(key_of[0], (ATOMS, C), 1.0, 6.0, ((0, 128),))
    frac = jnp.clip(1.0 * jax.random.uniform(key_of[1], (3, ATOMS), jnp.float32) ** steps_of(key_of[1], (3, ATOMS), ((1, 128),), -0.2, 0.2), 0.0, 1.0)
    neighbours = touch_ends(jax.random.randint(key_of[2], (K, ATOMS), 0, ATOMS_DEV + 9 * HALO_DEV), jax.random.fold_in(key_of[2], 1), 0, (ATOMS_DEV + 9 * HALO_DEV) - 1).astype(jnp.int32)
    nbr_mask = touch_ends((jax.random.randint(key_of[3], (K, ATOMS), 0, 8) < 7).astype(jnp.int32), jax.random.fold_in(key_of[3], 1), 0, 1)
    send_list = touch_ends(jax.random.randint(key_of[4], (HALO,), 0, ATOMS_DEV), jax.random.fold_in(key_of[4], 1), 0, ATOMS_DEV - 1).astype(jnp.int32)
    wavevectors = touch_ends(jax.random.randint(key_of[5], (3, MODES), -6, 7), jax.random.fold_in(key_of[5], 1), -6, 6).astype(jnp.int32)
    w_in = noise(key_of[6], (LAYERS, C, C), C ** -0.5, 0.5)
    w_filter1 = noise(key_of[7], (LAYERS, NR, C), (NR // 4) ** -0.5, 2.0)
    w_filter2 = noise(key_of[8], (LAYERS, C, C), C ** -0.5, 0.5)
    w_update1 = noise(key_of[9], (LAYERS, C, C), C ** -0.5, 0.5)
    w_update2 = noise(key_of[10], (LAYERS, C, C), C ** -0.5, 0.5)
    w_charge = noise(key_of[11], (C, Q), C ** -0.5, 0.5)
    screening = jnp.clip(jnp.exp(jax.random.uniform(key_of[12], (Q,), jnp.float32, math.log(1.0), math.log(64.0))), 1.0, 64.0)
    w_head = noise(key_of[13], (C, C), C ** -0.5, 0.5)
    w_potential = noise(key_of[14], (Q, C), Q ** -0.5, 1.5)
    w_energy = noise(key_of[15], (C,), C ** -0.5, 0.5)
    return dict(features=features, frac=frac, neighbours=neighbours, nbr_mask=nbr_mask, send_list=send_list, wavevectors=wavevectors, w_in=w_in, w_filter1=w_filter1, w_filter2=w_filter2, w_update1=w_update1, w_update2=w_update2, w_charge=w_charge, screening=screening, w_head=w_head, w_potential=w_potential, w_energy=w_energy)


two_pi = 2.0 * math.pi
ewald_width = 64.0

def radial_basis(chord_sq, basis_count):
    spacing = 3.0 / (basis_count - 1)
    centres = jnp.arange(basis_count, dtype=jnp.float32) * spacing
    scaled = (chord_sq[..., None] - centres) / spacing
    return jnp.exp(-0.5 * scaled * scaled).astype(jnp.bfloat16)

def mode_phases(coords, wave_block):
    angles = two_pi * (coords[0][:, None] * wave_block[0][None, :] + coords[1][:, None] * wave_block[1][None, :] + coords[2][:, None] * wave_block[2][None, :])
    return (jnp.cos(angles).astype(jnp.bfloat16), jnp.sin(angles).astype(jnp.bfloat16))

def responses(sums, wave_float, screening):
    norm_sq = lax.optimization_barrier(jnp.sum(wave_float * wave_float, axis=0))
    kernel = jnp.exp(-norm_sq / ewald_width)[None, :] / (norm_sq[None, :] + screening[:, None])
    latent = screening.shape[0]
    return jnp.concatenate([kernel * sums[:latent], kernel * sums[latent:]], axis=0).astype(jnp.bfloat16)

def padded_grid(values, send_list):
    width = values.shape[-1]
    blocks = values.reshape(N_GX, N_YZ, ATOMS_DEV, width)
    chosen = send_list.reshape(N_GX, N_YZ, HALO_DEV)
    sent_rows = jnp.take_along_axis(blocks, chosen[:, :, :, None], axis=2)
    sent_rows = sent_rows.reshape(N_GX, N_YZ, HALO_SIDE, HALO_SIDE, width).transpose(0, 2, 1, 3, 4)
    send_grid = sent_rows.reshape(N_GX * HALO_SIDE, N_YZ * HALO_SIDE, width)
    return jnp.pad(send_grid, ((HALO_SIDE, HALO_SIDE), (HALO_SIDE, HALO_SIDE), (0, 0)), mode='wrap')

def window_rows(grid, device):
    row_start = (device // N_YZ * HALO_SIDE).astype(jnp.int32)
    col_start = (device % N_YZ * HALO_SIDE).astype(jnp.int32)
    window = lax.dynamic_slice(grid, (row_start, col_start, jnp.int32(0)), (3 * HALO_SIDE, 3 * HALO_SIDE, grid.shape[2]))
    return window.reshape(9 * HALO_DEV, grid.shape[2])

def reference(features, frac, neighbours, nbr_mask, send_list, wavevectors, w_in, w_filter1, w_filter2, w_update1, w_update2, w_charge, screening, w_head, w_potential, w_energy):
    blocks_total = N_GX * N_YZ
    device_ids = jnp.arange(blocks_total, dtype=jnp.int32)
    frac_blocks = frac.reshape(3, blocks_total, ATOMS_DEV).transpose(1, 0, 2)
    nbr_blocks = neighbours.reshape(K, blocks_total, ATOMS_DEV).transpose(1, 0, 2)
    mask_blocks = nbr_mask.reshape(K, blocks_total, ATOMS_DEV).transpose(1, 0, 2)
    pos_grid = padded_grid(frac.T, send_list)
    state = features
    for layer_index in range(LAYERS):
        projected = jnp.dot(state, w_in[layer_index], preferred_element_type=jnp.float32).astype(jnp.bfloat16)
        msg_grid = padded_grid(projected, send_list)
        first_w = w_filter1[layer_index].astype(jnp.float32)
        second_w = w_filter2[layer_index].astype(jnp.float32)

        def per_device(device):
            own_frac = frac_blocks[device]
            pos_table = jnp.concatenate([own_frac, window_rows(pos_grid, device).T], axis=1)
            slot_ids = nbr_blocks[device]
            others = jnp.take(pos_table, slot_ids, axis=1)
            sines = jnp.sin(math.pi * (others - own_frac[:, None, :]))
            chord_sq = lax.optimization_barrier(jnp.sum(sines * sines, axis=0))
            radial = radial_basis(chord_sq, NR)
            filter_hidden = jax.nn.silu(jnp.einsum('kbr,rc->kbc', radial.astype(jnp.float32), first_w)).astype(jnp.bfloat16)
            filters = jnp.einsum('kbc,cd->kbd', filter_hidden.astype(jnp.float32), second_w)
            own_rows = lax.dynamic_slice_in_dim(projected, (device * ATOMS_DEV).astype(jnp.int32), ATOMS_DEV, 0)
            slot_table = jnp.concatenate([own_rows, window_rows(msg_grid, device)], axis=0)
            sources = jnp.take(slot_table, slot_ids, axis=0)
            message = filters * sources.astype(jnp.float32) * mask_blocks[device][..., None].astype(jnp.float32)
            return (lax.optimization_barrier(jnp.sum(message, axis=0)) * (1.0 / math.sqrt(K))).astype(jnp.bfloat16)
        aggregate = lax.map(per_device, device_ids).reshape(ATOMS, C)
        update = jax.nn.silu(jnp.dot(aggregate, w_update1[layer_index], preferred_element_type=jnp.float32)).astype(jnp.bfloat16)
        state = (state.astype(jnp.float32) + jnp.dot(update, w_update2[layer_index], preferred_element_type=jnp.float32)).astype(jnp.bfloat16)
    charges = lax.dot_general(w_charge, state, (((0,), (1,)), ((), ())), preferred_element_type=jnp.float32).astype(jnp.bfloat16)
    charge_blocks = charges.reshape(Q, blocks_total, ATOMS_DEV).transpose(1, 0, 2)
    wave_all = wavevectors.astype(jnp.float32)
    mode_block = min(256, MODES)
    mode_turns = MODES // mode_block
    mode_starts = jnp.arange(mode_turns, dtype=jnp.int32) * mode_block

    def device_sums(total, device):
        own_frac = frac_blocks[device]
        own_charge = charge_blocks[device]

        def one_block(offset):
            wave_block = lax.dynamic_slice_in_dim(wave_all, offset, mode_block, 1)
            cos_part, sine_part = mode_phases(own_frac, wave_block)
            return jnp.concatenate([jnp.dot(own_charge, cos_part, preferred_element_type=jnp.float32), jnp.dot(own_charge, sine_part, preferred_element_type=jnp.float32)], axis=0)
        stacked = lax.map(one_block, mode_starts)
        return (total + stacked.transpose(1, 0, 2).reshape(2 * Q, MODES), None)
    sums, unused = lax.scan(device_sums, jnp.zeros((2 * Q, MODES), jnp.float32), device_ids)
    answer = responses(sums, wave_all, screening)
    contract = (((1,), (1,)), ((), ()))

    def device_field(device):
        own_frac = frac_blocks[device]

        def potential_step(turn, running):
            offset = (turn * mode_block).astype(jnp.int32)
            wave_block = lax.dynamic_slice_in_dim(wave_all, offset, mode_block, 1)
            cos_part, sine_part = mode_phases(own_frac, wave_block)
            resp_block = lax.dynamic_slice_in_dim(answer, offset, mode_block, 1)
            return running + lax.dot_general(resp_block[:Q], cos_part, contract, preferred_element_type=jnp.float32) + lax.dot_general(resp_block[Q:], sine_part, contract, preferred_element_type=jnp.float32)
        return lax.fori_loop(0, mode_turns, potential_step, jnp.zeros((Q, ATOMS_DEV), jnp.float32))
    field = lax.map(device_field, device_ids).transpose(1, 0, 2).reshape(Q, ATOMS)
    potentials = field * (4.0 / math.sqrt(ATOMS))
    potential_input = potentials.astype(jnp.bfloat16)
    summed = jnp.dot(state, w_head, preferred_element_type=jnp.float32) + lax.dot_general(potential_input, w_potential, (((0,), (0,)), ((), ())), preferred_element_type=jnp.float32)
    readout = jax.nn.silu(summed).astype(jnp.bfloat16)
    energies = jnp.dot(readout, w_energy, preferred_element_type=jnp.float32)
    return (state, potentials, energies)
```

```python
import functools
import math

import jax
import jax.numpy as jnp
from jax import lax
from jax.experimental import pallas as pl
from jax.experimental.pallas import tpu as pltpu
from jax.sharding import PartitionSpec as P

C = 128
NR = 32
Q = 16
K = 32
SIDE = 16
T = 512
H = 256
PACK = H + 32
SLOTS = T + 9 * H
ZERO = SLOTS
PIECES = SLOTS // 128
KX = 7
YZ = 13
BETA = 176
ROWS = KX * Q
SUM_ROWS = ROWS + 16
SUM_LANES = 384
f32, bf16, i32 = jnp.float32, jnp.bfloat16, jnp.int32


def rows_of(shape, dim):
    return lax.broadcasted_iota(i32, shape, dim)


def dot(a, b, dims=((1,), (0,))):
    return lax.dot_general(a, b, (dims, ((), ())), preferred_element_type=f32)


def silu(v):
    half = 0.5 * v
    return half + half * jnp.tanh(half)


def sin_pi(x):
    y = x * x
    total = jnp.full_like(x, math.pi**13 / math.factorial(13))
    for order in (11, 9, 7, 5, 3, 1):
        sign = -1.0 if order % 4 == 3 else 1.0
        total = total * y + sign * math.pi**order / math.factorial(order)
    return total * x


def pick8(table, index_of):
    sub = rows_of((8, C), 0)
    picked = table[pl.ds(index_of(0), 8, stride=0), :]
    for j in range(1, 8):
        picked = jnp.where(sub == j, table[pl.ds(index_of(j), 8, stride=0), :], picked)
    return picked


def pick_send_rows(table, send, out):
    def group(g, carry):
        base = g * 16
        low = pick8(table, lambda j: send[base + j])
        high = pick8(table, lambda j: send[base + 8 + j])
        out[pl.ds(pl.multiple_of(base, 16), 16), :] = jnp.concatenate([low, high], axis=0).astype(bf16)
        return carry

    lax.fori_loop(0, H // 16, group, 0)


def first_kernel(send, send_lanes, features, frac, w_in, proj_out, out, table, parts):
    projected = dot(features[...], w_in[0]).astype(bf16)
    proj_out[...] = projected
    table[...] = projected.astype(f32)
    pick_send_rows(table, send, out)
    parts[...] = jnp.zeros_like(parts)
    for half in range(2):
        index = jnp.broadcast_to(send_lanes[half : half + 1, :], (8, 128))
        low, high = index & 127, index >> 7
        for c in range(3):
            value = jnp.zeros((8, 128), f32)
            for p in range(T // 128):
                source = jnp.broadcast_to(frac[c : c + 1, p * 128 : (p + 1) * 128], (8, 128))
                value = jnp.where(high == p, jnp.take_along_axis(source, low, axis=1), value)
            value = value[0:1]
            for part in range(3):
                rounded = value.astype(bf16).astype(f32)
                row = part * 8 + half * 4 + c
                parts[row : row + 1, :] = rounded
                value = value - rounded
    out[H:PACK, :] = parts[...].astype(bf16)


def prepare_kernel(neighbours, mask, frac, waves, slots_out, phase_out, axis_out, digits_out, plane):
    u = neighbours[...] - T
    row = (u * 43691) >> 21
    col = u - row * 48
    block = (col >> 4) * 3 + (row >> 4)
    moved = T + block * H + (row & 15) * SIDE + (col & 15)
    slots = jnp.where(mask[...] != 0, jnp.where(u < 0, u + T, moved), ZERO)
    for b in range(T // 128):
        slots_out[b * K : (b + 1) * K, :] = slots[:, b * 128 : (b + 1) * 128]

    def turn(c):
        harmonics = []
        for n in range(KX):
            x = frac[c : c + 1, :] * float(n)
            x = x - jnp.floor(x + 0.5)
            s = sin_pi(jnp.clip(2.0 * x - jnp.floor(2.0 * x + 0.5), -0.5, 0.5))
            odd = (jnp.floor(2.0 * x + 0.5).astype(i32) & 1) != 0
            sine = jnp.where(odd, -s, s)
            y = 2.0 * x + 0.5
            t = y - jnp.floor(y + 0.5)
            s2 = sin_pi(jnp.clip(t, -0.5, 0.5))
            odd2 = (jnp.floor(y + 0.5).astype(i32) & 1) != 0
            cosine = jnp.where(odd2, -s2, s2)
            harmonics.append((cosine, sine))
        return harmonics

    hx, hy, hz = turn(0), turn(1), turn(2)
    axis_out[...] = jnp.zeros_like(axis_out)
    for n in range(KX):
        axis_out[n : n + 1, :] = hx[n][0]
        axis_out[8 + n : 9 + n, :] = hx[n][1]

    def signed(h, k):
        c, s = h[abs(k)]
        return (c, s) if k >= 0 else (c, -s)

    zc = jnp.concatenate([signed(hz, k)[0] for k in range(-6, 7)], axis=0)
    zs = jnp.concatenate([signed(hz, k)[1] for k in range(-6, 7)], axis=0)
    plane[...] = jnp.zeros_like(plane)
    for n in range(YZ):
        yc, ys = signed(hy, n - 6)
        c = yc * zc - ys * zs
        s = ys * zc + yc * zs
        plane[0, n * YZ : (n + 1) * YZ, :] = c
        plane[1, n * YZ : (n + 1) * YZ, :] = s
    phase_out[:BETA, :T] = plane[0].astype(bf16)
    phase_out[:BETA, T:] = (-plane[1]).astype(bf16)
    phase_out[BETA:, :T] = plane[1].astype(bf16)
    phase_out[BETA:, T:] = plane[0].astype(bf16)

    modes = waves.shape[1]
    flip = jnp.where(waves[0:1, :] < 0, -1, 1)
    kx = waves[0:1, :] * flip
    beta = (waves[1:2, :] * flip + 6) * YZ + waves[2:3, :] * flip + 6
    hot_x = (rows_of((8, modes), 0) == kx).astype(f32).astype(bf16)
    r = rows_of((SUM_LANES, modes), 0)
    r = jnp.where(r >= BETA, r - BETA, r)
    hot_b = (r == beta).astype(f32).astype(bf16)
    count = dot(hot_x, hot_b, ((1,), (1,))).astype(i32)
    thirds = [count]
    for _ in range(3):
        thirds.append((thirds[-1] * 171) >> 9)
    digit = [a - 3 * b for a, b in zip(thirds[:3], thirds[1:])] + [thirds[3]]
    lane = rows_of((8, SUM_LANES), 1)
    first = lane < BETA
    keep = lane < 2 * BETA
    low = jnp.where(first, digit[0], digit[2])
    high = jnp.where(first, digit[1], digit[3])
    digits_out[0:8, :] = jnp.where(keep, low, 0).astype(f32)
    digits_out[8:16, :] = jnp.where(keep, high, 0).astype(f32)


def fill_table(table, projected, rows_in, stride):
    table[0:T, :] = projected[...].astype(f32)
    for by in range(3):
        for bx in range(3):
            at = T + (by * 3 + bx) * H
            table[at : at + H, :] = rows_in[by][bx * stride : bx * stride + H, :].astype(f32)
    table[ZERO : ZERO + 8, :] = jnp.zeros((8, C), f32)


def fill_filter_weights(w1, w2, layer, wide1, wide2):
    wide1[...] = jnp.zeros_like(wide1)
    wide2[...] = jnp.zeros_like(wide2)
    for j in range(4):
        wide1[j * NR : (j + 1) * NR, j * C : (j + 1) * C] = w1[layer]
    for j in range(2):
        wide2[j * C : (j + 1) * C, j * C : (j + 1) * C] = w2[layer]


def filters_of(chord_rows, wide1, wide2):
    inv_width = 31.0 / 3.0
    centre = rows_of((NR, 128), 0).astype(f32)
    radial = []
    for chord in chord_rows:
        scaled = chord * inv_width - centre
        radial.append(jnp.exp(-0.5 * scaled * scaled))
    radial = jnp.concatenate(radial, axis=0).astype(bf16)
    hidden = silu(dot(radial, wide1[...], ((0,), (0,)))).astype(bf16)
    return (dot(hidden[:, : 2 * C], wide2[...]), dot(hidden[:, 2 * C :], wide2[...]))


def update_tail(total, state, w_update1, w_update2, layer):
    aggregate = (total[...] * (1.0 / math.sqrt(K))).astype(bf16)
    update = silu(dot(aggregate, w_update1[layer])).astype(bf16)
    return (state[...].astype(f32) + dot(update, w_update2[layer])).astype(bf16)


def chords(slots, frac, rows_in, chord, places):
    for c in range(3):
        for p in range(T // 128):
            places[c * 24 + p : c * 24 + p + 1, :] = frac[c : c + 1, p * 128 : (p + 1) * 128]
    for by in range(3):
        for bx in range(3):
            part = rows_in[by][bx * PACK + H : (bx + 1) * PACK, :].astype(f32)
            value = part[0:8] + part[8:16] + part[16:24]
            for half in range(2):
                p = T // 128 + (by * 3 + bx) * 2 + half
                for c in range(3):
                    at = c * 24 + p
                    places[at : at + 1, :] = value[half * 4 + c : half * 4 + c + 1]

    def lane_block(b, carry):
        lanes = pl.ds(pl.multiple_of(b * 128, 128), 128)
        for g in range(K // 8):
            index = slots[pl.ds(pl.multiple_of(b * K + g * 8, 8), 8), :]
            low, high = index & 127, index >> 7
            total = jnp.zeros((8, 128), f32)
            value = [jnp.zeros((8, 128), f32) for _ in range(3)]
            for p in range(PIECES):
                here = high == p
                for c in range(3):
                    source = places[pl.ds(c * 24 + p, 8, stride=0), :]
                    value[c] = jnp.where(here, jnp.take_along_axis(source, low, axis=1), value[c])
            for c in range(3):
                apart = value[c] - frac[c : c + 1, lanes]
                apart = apart - jnp.floor(apart + 0.5)
                sine = sin_pi(apart)
                total = total + sine * sine
            chord[pl.ds(pl.multiple_of(b * K + g * 8, 8), 8), :] = total
        return carry

    lax.fori_loop(0, T // 128, lane_block, 0)


def add_messages(table, slots, filters, total, block, group):
    first = block * (K * 128) + group * 512
    for g in range(16):
        start = block * 128 + g * 8
        at = pl.ds(pl.multiple_of(start, 8), 8)
        acc = total[at, :]
        for j in range(4):
            source = pick8(table, lambda s: slots[first + (j * 128 + g * 8 + s)])
            acc = acc + source * filters[g * 8 : g * 8 + 8, j * C : (j + 1) * C]
        total[at, :] = acc


def layer_kernel(
    slots_s, send, slots, frac, x_low, x_own, x_high, projected, state,
    w1, w2, w_update1, w_update2, w_in,
    state_out, proj_out, send_out, chord_out,
    table, places, wide1, wide2, ping, pong, total, proj_table,
):
    rows_in = (x_low, x_own, x_high)
    fill_table(table, projected, rows_in, PACK)
    fill_filter_weights(w1, w2, 0, wide1, wide2)
    chords(slots, frac, rows_in, chord_out, places)
    total[...] = jnp.zeros_like(total)

    def make(step, buffer):
        block, group = step // 8, step % 8
        rows = [chord_out[pl.ds(block * K + group * 4 + j, NR, stride=0), :] for j in range(4)]
        a, b = filters_of(rows, wide1, wide2)
        buffer[:, : 2 * C] = a
        buffer[:, 2 * C :] = b

    def use(step, buffer):
        add_messages(table, slots_s, buffer, total, step // 8, step % 8)

    make(0, ping)

    def pair(i, carry):
        make(2 * i + 1, pong)
        use(2 * i, ping)
        make(jnp.minimum(2 * i + 2, 31), ping)
        use(2 * i + 1, pong)
        return carry

    lax.fori_loop(0, 16, pair, 0)
    new_state = update_tail(total, state, w_update1, w_update2, 0)
    state_out[...] = new_state
    projected1 = dot(new_state, w_in[1]).astype(bf16)
    proj_out[...] = projected1
    proj_table[...] = projected1.astype(f32)
    pick_send_rows(proj_table, send, send_out)


def filter_kernel(chord, w1, w2, out, wide1, wide2):
    @pl.when(pl.program_id(0) == 0)
    def _():
        fill_filter_weights(w1, w2, 1, wide1, wide2)

    first = pl.program_id(0) * K

    def group(g, carry):
        rows = [chord[pl.ds(first + g * 4 + j, NR, stride=0), :] for j in range(4)]
        a, b = filters_of(rows, wide1, wide2)
        out[g, :, : 2 * C] = a.astype(bf16)
        out[g, :, 2 * C :] = b.astype(bf16)
        return carry

    lax.fori_loop(0, 8, group, 0)


def last_layer_kernel(
    slots_s, filters, x_low, x_own, x_high, projected, state,
    w_update1, w_update2, w_charge, phase, axis, digits,
    state_out, sums_out,
    table, total, left,
):
    block = pl.program_id(0)

    @pl.when(block == 0)
    def _():
        fill_table(table, projected, (x_low, x_own, x_high), H)
        total[...] = jnp.zeros_like(total)

    def group(g, carry):
        add_messages(table, slots_s, filters.at[g], total, block, g)
        return carry

    lax.fori_loop(0, 8, group, 0)

    @pl.when(block == T // 128 - 1)
    def _():
        new_state = update_tail(total, state, w_update1, w_update2, 1)
        state_out[...] = new_state
        charges = dot(w_charge[...], new_state, ((0,), (1,))).astype(bf16).astype(f32)
        for n in range(KX):
            left[n * Q : (n + 1) * Q, :T] = (charges * axis[n : n + 1, :]).astype(bf16)
            left[n * Q : (n + 1) * Q, T:] = (charges * axis[8 + n : 9 + n, :]).astype(bf16)
        sums_out[...] = jnp.zeros_like(sums_out)
        sums_out[:ROWS, : 2 * BETA] = dot(left[...], phase[...], ((1,), (1,))).astype(bf16)
        sums_out[ROWS:, :] = digits[...].astype(bf16)


def field_kernel(
    sums, phase, axis, screening, state, w_head, w_potential, w_energy,
    potentials_out, energies_out, response,
):
    lane = rows_of((1, SUM_LANES), 1)
    beta = jnp.where(lane >= BETA, lane - BETA, lane)
    y = (beta * 79) >> 10
    ky = y - 6
    kz = beta - y * YZ - 6
    plane_sq = (ky * ky + kz * kz).astype(f32)
    digits = sums[ROWS:, :].astype(f32)
    packed = digits[0:8] + 3.0 * digits[8:16]
    ahead = pltpu.roll(packed, SUM_LANES - BETA, 1)
    behind = pltpu.roll(packed, BETA, 1)
    lane8 = rows_of((8, SUM_LANES), 1)
    count = jnp.where(lane8 < BETA, packed + 9.0 * ahead, behind + 9.0 * packed)
    square = rows_of((Q, Q), 0) == rows_of((Q, Q), 1)
    screen = jnp.sum(jnp.where(square, jnp.broadcast_to(screening[...], (Q, Q)), 0.0), axis=1, keepdims=True)
    for n in range(KX):
        norm_sq = plane_sq + float(n * n)
        kernel = jnp.exp(norm_sq * (-1.0 / 64.0)) * count[n : n + 1, :] / (norm_sq + screen)
        value = kernel * sums[n * Q : (n + 1) * Q, :].astype(f32)
        response[n * Q : (n + 1) * Q, :] = value[:, : 2 * BETA].astype(bf16)
    field = dot(response[...], phase[...])
    total = jnp.zeros((Q, T), f32)
    for n in range(KX):
        part = field[n * Q : (n + 1) * Q]
        total = total + part[:, :T] * axis[n : n + 1, :] + part[:, T:] * axis[8 + n : 9 + n, :]
    potentials = total * (4.0 / 256.0)
    potentials_out[...] = potentials
    summed = dot(state[...], w_head[...]) + dot(potentials.astype(bf16), w_potential[...], ((0,), (0,)))
    readout = silu(summed).astype(bf16)
    energies_out[...] = dot(w_energy[...], readout, ((1,), (1,)))


VMEM = pl.BlockSpec(memory_space=pltpu.VMEM)
SMEM = pl.BlockSpec(memory_space=pltpu.SMEM)


def shape(*dims, dtype=f32):
    return jax.ShapeDtypeStruct(dims, dtype)


def call(kernel, ins, outs, scratch, flops, moved):
    return pl.pallas_call(
        kernel,
        out_shape=outs,
        in_specs=ins,
        out_specs=jax.tree.map(lambda _: VMEM, outs),
        scratch_shapes=scratch,
        cost_estimate=pl.CostEstimate(flops=flops, bytes_accessed=moved, transcendentals=0),
    )


def halo(block):
    for axis in ("gx", "yz"):
        count = lax.axis_size(axis)
        forward = [(i, (i + 1) % count) for i in range(count)]
        backward = [(target, source) for source, target in forward]
        low = lax.ppermute(block, axis, forward)
        high = lax.ppermute(block, axis, backward)
        if axis == "gx":
            block = jnp.concatenate([low, block, high], axis=0)
    return low, block, high


STAGES = (("yz", (1, 2, 3)), ("yz", (4, 8, 12)), ("gx", (1, 2, 3)), ("gx", (4,)))


def sum_everywhere(part):
    for axis, offsets in STAGES:
        count = lax.axis_size(axis)
        taken = [lax.ppermute(part, axis, [(i, i ^ o) for i in range(count)]) for o in offsets]
        total = part.astype(f32)
        for one in taken:
            total = total + one.astype(f32)
        part = total.astype(bf16)
    return part


def shards(
    features, frac, neighbours, nbr_mask, send_list, wavevectors, w_in, w_filter1, w_filter2,
    w_update1, w_update2, w_charge, screening, w_head, w_potential, w_energy,
):
    projected, sent = call(
        first_kernel, [SMEM, VMEM, VMEM, VMEM, VMEM],
        (shape(T, C, dtype=bf16), shape(PACK, C, dtype=bf16)),
        [pltpu.VMEM((T, C), f32), pltpu.VMEM((32, 128), f32)], 20_000_000, 300_000,
    )(send_list, send_list.reshape(2, 128), features, frac, w_in)
    slots, phase, axis, digits = call(
        prepare_kernel, [VMEM] * 4,
        (shape(4 * K, 128, dtype=i32), shape(2 * BETA, 2 * T, dtype=bf16), shape(16, T), shape(16, SUM_LANES)),
        [pltpu.VMEM((2, BETA, T), f32)], 2_000_000_000, 4_000_000,
    )(neighbours, nbr_mask, frac, wavevectors)
    x_low, x_own, x_high = halo(sent)
    state, projected, sent, chord = call(
        layer_kernel, [SMEM, SMEM] + [VMEM] * 12,
        (shape(T, C, dtype=bf16), shape(T, C, dtype=bf16), shape(H, C, dtype=bf16), shape(4 * K, 128)),
        [
            pltpu.VMEM((SLOTS + 8, C), f32), pltpu.VMEM((72, 128), f32),
            pltpu.VMEM((4 * NR, 4 * C), bf16), pltpu.VMEM((2 * C, 2 * C), bf16),
            pltpu.VMEM((128, 4 * C), f32), pltpu.VMEM((128, 4 * C), f32),
            pltpu.VMEM((T, C), f32), pltpu.VMEM((T, C), f32),
        ], 4_000_000_000, 4_000_000,
    )(
        slots.reshape(-1), send_list, slots, frac, x_low, x_own, x_high, projected, features,
        w_filter1, w_filter2, w_update1, w_update2, w_in,
    )
    x_low, x_own, x_high = halo(sent)
    whole = lambda a: pl.BlockSpec(a.shape, lambda i: (0,) * a.ndim)
    block = pl.BlockSpec((8, 128, 4 * C), lambda i: (i, 0, 0))
    filters = pl.pallas_call(
        filter_kernel, grid=(T // 128,),
        out_shape=shape(32, 128, 4 * C, dtype=bf16),
        in_specs=[whole(chord), whole(w_filter1), whole(w_filter2)], out_specs=block,
        scratch_shapes=[pltpu.VMEM((4 * NR, 4 * C), bf16), pltpu.VMEM((2 * C, 2 * C), bf16)],
        cost_estimate=pl.CostEstimate(flops=4_000_000_000, bytes_accessed=8_000_000, transcendentals=0),
    )(chord, w_filter1, w_filter2)
    rest = (x_low, x_own, x_high, projected, state, w_update1, w_update2, w_charge, phase, axis, digits)
    embeddings, sums = pl.pallas_call(
        last_layer_kernel, grid=(T // 128,),
        out_shape=(shape(T, C, dtype=bf16), shape(SUM_ROWS, SUM_LANES, dtype=bf16)),
        in_specs=[SMEM, block] + [whole(a) for a in rest],
        out_specs=(pl.BlockSpec((T, C), lambda i: (0, 0)), pl.BlockSpec((SUM_ROWS, SUM_LANES), lambda i: (0, 0))),
        scratch_shapes=[pltpu.VMEM((SLOTS + 8, C), f32), pltpu.VMEM((T, C), f32), pltpu.VMEM((ROWS, 2 * T), bf16)],
        cost_estimate=pl.CostEstimate(flops=1_000_000_000, bytes_accessed=8_000_000, transcendentals=0),
    )(slots.reshape(-1), filters, *rest)
    sums = sum_everywhere(sums)
    potentials, energies = call(
        field_kernel, [VMEM] * 8, (shape(Q, T), shape(1, T)),
        [pltpu.VMEM((ROWS, 2 * BETA), bf16)], 100_000_000, 2_000_000,
    )(
        sums, phase, axis, screening.reshape(1, Q), embeddings, w_head, w_potential,
        w_energy.reshape(1, C),
    )
    return embeddings, potentials, energies.reshape(T)


def solution(mesh):
    atoms = ("gx", "yz")
    return jax.shard_map(
        shards,
        mesh=mesh,
        in_specs=(P(atoms, None), P(None, atoms), P(None, atoms), P(None, atoms), P(atoms), P(None, atoms))
        + (P(),) * 10,
        out_specs=(P(atoms, None), P(None, atoms), P(atoms)),
        check_vma=False,
    )
```

```python
import functools
import math

import jax
import jax.numpy as jnp
from jax import lax
from jax.experimental import pallas as pl
from jax.experimental.pallas import tpu as pltpu
from jax.sharding import PartitionSpec as P

C = 128
NR = 32
Q = 16
K = 32
SIDE = 16
T = 512
H = 256
PACK = H + 32
SLOTS = T + 9 * H
ZERO = SLOTS
PIECES = SLOTS // 128
KX = 7
YZ = 13
BETA = 176
ROWS = KX * Q
SUM_ROWS = ROWS + 16
SUM_LANES = 384
HALF = SUM_ROWS // 2
f32, bf16, i32 = jnp.float32, jnp.bfloat16, jnp.int32


def rows_of(shape, dim):
    return lax.broadcasted_iota(i32, shape, dim)


def dot(a, b, dims=((1,), (0,))):
    return lax.dot_general(a, b, (dims, ((), ())), preferred_element_type=f32)


def silu(v):
    half = 0.5 * v
    return half + half * jnp.tanh(half)


def sin_pi(x):
    y = x * x
    total = jnp.full_like(x, math.pi**13 / math.factorial(13))
    for order in (11, 9, 7, 5, 3, 1):
        sign = -1.0 if order % 4 == 3 else 1.0
        total = total * y + sign * math.pi**order / math.factorial(order)
    return total * x


def pick8(table, index_of):
    sub = rows_of((8, C), 0)
    picked = table[pl.ds(index_of(0), 8, stride=0), :]
    for j in range(1, 8):
        picked = jnp.where(sub == j, table[pl.ds(index_of(j), 8, stride=0), :], picked)
    return picked


def pick_send_rows(table, send, out):
    def group(g, carry):
        base = g * 16
        low = pick8(table, lambda j: send[base + j])
        high = pick8(table, lambda j: send[base + 8 + j])
        out[pl.ds(pl.multiple_of(base, 16), 16), :] = jnp.concatenate([low, high], axis=0).astype(bf16)
        return carry

    lax.fori_loop(0, H // 16, group, 0)


def first_kernel(send, send_lanes, features, frac, w_in, proj_out, out, table, parts):
    projected = dot(features[...], w_in[0]).astype(bf16)
    proj_out[...] = projected
    table[...] = projected.astype(f32)
    pick_send_rows(table, send, out)
    parts[...] = jnp.zeros_like(parts)
    for half in range(2):
        index = jnp.broadcast_to(send_lanes[half : half + 1, :], (8, 128))
        low, high = index & 127, index >> 7
        for c in range(3):
            value = jnp.zeros((8, 128), f32)
            for p in range(T // 128):
                source = jnp.broadcast_to(frac[c : c + 1, p * 128 : (p + 1) * 128], (8, 128))
                value = jnp.where(high == p, jnp.take_along_axis(source, low, axis=1), value)
            value = value[0:1]
            for part in range(3):
                rounded = value.astype(bf16).astype(f32)
                row = part * 8 + half * 4 + c
                parts[row : row + 1, :] = rounded
                value = value - rounded
    out[H:PACK, :] = parts[...].astype(bf16)


def prepare_kernel(neighbours, mask, frac, waves, slots_out, phase_out, axis_out, digits_out, plane):
    u = neighbours[...] - T
    row = (u * 43691) >> 21
    col = u - row * 48
    block = (col >> 4) * 3 + (row >> 4)
    moved = T + block * H + (row & 15) * SIDE + (col & 15)
    slots = jnp.where(mask[...] != 0, jnp.where(u < 0, u + T, moved), ZERO)
    for b in range(T // 128):
        slots_out[b * K : (b + 1) * K, :] = slots[:, b * 128 : (b + 1) * 128]

    def turn(c):
        harmonics = []
        for n in range(KX):
            x = frac[c : c + 1, :] * float(n)
            x = x - jnp.floor(x + 0.5)
            s = sin_pi(jnp.clip(2.0 * x - jnp.floor(2.0 * x + 0.5), -0.5, 0.5))
            odd = (jnp.floor(2.0 * x + 0.5).astype(i32) & 1) != 0
            sine = jnp.where(odd, -s, s)
            y = 2.0 * x + 0.5
            t = y - jnp.floor(y + 0.5)
            s2 = sin_pi(jnp.clip(t, -0.5, 0.5))
            odd2 = (jnp.floor(y + 0.5).astype(i32) & 1) != 0
            cosine = jnp.where(odd2, -s2, s2)
            harmonics.append((cosine, sine))
        return harmonics

    hx, hy, hz = turn(0), turn(1), turn(2)
    axis_out[...] = jnp.zeros_like(axis_out)
    for n in range(KX):
        axis_out[n : n + 1, :] = hx[n][0]
        axis_out[8 + n : 9 + n, :] = hx[n][1]

    def signed(h, k):
        c, s = h[abs(k)]
        return (c, s) if k >= 0 else (c, -s)

    zc = jnp.concatenate([signed(hz, k)[0] for k in range(-6, 7)], axis=0)
    zs = jnp.concatenate([signed(hz, k)[1] for k in range(-6, 7)], axis=0)
    plane[...] = jnp.zeros_like(plane)
    for n in range(YZ):
        yc, ys = signed(hy, n - 6)
        c = yc * zc - ys * zs
        s = ys * zc + yc * zs
        plane[0, n * YZ : (n + 1) * YZ, :] = c
        plane[1, n * YZ : (n + 1) * YZ, :] = s
    phase_out[:BETA, :T] = plane[0].astype(bf16)
    phase_out[:BETA, T:] = (-plane[1]).astype(bf16)
    phase_out[BETA:, :T] = plane[1].astype(bf16)
    phase_out[BETA:, T:] = plane[0].astype(bf16)

    modes = waves.shape[1]
    flip = jnp.where(waves[0:1, :] < 0, -1, 1)
    kx = waves[0:1, :] * flip
    beta = (waves[1:2, :] * flip + 6) * YZ + waves[2:3, :] * flip + 6
    hot_x = (rows_of((8, modes), 0) == kx).astype(f32).astype(bf16)
    r = rows_of((SUM_LANES, modes), 0)
    r = jnp.where(r >= BETA, r - BETA, r)
    hot_b = (r == beta).astype(f32).astype(bf16)
    count = dot(hot_x, hot_b, ((1,), (1,))).astype(i32)
    thirds = [count]
    for _ in range(3):
        thirds.append((thirds[-1] * 171) >> 9)
    digit = [a - 3 * b for a, b in zip(thirds[:3], thirds[1:])] + [thirds[3]]
    lane = rows_of((8, SUM_LANES), 1)
    first = lane < BETA
    keep = lane < 2 * BETA
    low = jnp.where(first, digit[0], digit[2])
    high = jnp.where(first, digit[1], digit[3])
    digits_out[0:8, :] = jnp.where(keep, low, 0).astype(f32)
    digits_out[8:16, :] = jnp.where(keep, high, 0).astype(f32)


def fill_table(table, projected, rows_in, stride):
    table[0:T, :] = projected[...].astype(f32)
    for by in range(3):
        for bx in range(3):
            at = T + (by * 3 + bx) * H
            table[at : at + H, :] = rows_in[by][bx * stride : bx * stride + H, :].astype(f32)
    table[ZERO : ZERO + 8, :] = jnp.zeros((8, C), f32)


def fill_filter_weights(w1, w2, layer, wide1, wide2):
    wide1[...] = jnp.zeros_like(wide1)
    wide2[...] = jnp.zeros_like(wide2)
    for j in range(4):
        wide1[j * NR : (j + 1) * NR, j * C : (j + 1) * C] = w1[layer]
    for j in range(2):
        wide2[j * C : (j + 1) * C, j * C : (j + 1) * C] = w2[layer]


def radial_of(chord):
    scaled = chord * (31.0 / 3.0) - rows_of((NR, 128), 0).astype(f32)
    return jnp.exp(-0.5 * scaled * scaled).astype(bf16)


def make_filters(chord, group, wide1, wide2, out):
    radial = jnp.concatenate(
        [
            jnp.concatenate(
                [radial_of(chord[pl.ds(b * K + group * 4 + j, NR, stride=0), :]) for b in range(T // 128)], axis=1
            )
            for j in range(4)
        ],
        axis=0,
    )
    for h in range(2):
        hidden = silu(dot(radial, wide1[:, h * 2 * C : (h + 1) * 2 * C], ((0,), (0,)))).astype(bf16)
        out[h] = dot(hidden, wide2[...]).astype(bf16)


def update_tail(total, state, w_update1, w_update2, layer):
    aggregate = (total[...] * (1.0 / math.sqrt(K))).astype(bf16)
    update = silu(dot(aggregate, w_update1[layer])).astype(bf16)
    return (state[...].astype(f32) + dot(update, w_update2[layer])).astype(bf16)


def chords(slots, frac, rows_in, chord, places):
    for c in range(3):
        for p in range(T // 128):
            places[c * 24 + p : c * 24 + p + 1, :] = frac[c : c + 1, p * 128 : (p + 1) * 128]
    for by in range(3):
        for bx in range(3):
            part = rows_in[by][bx * PACK + H : (bx + 1) * PACK, :].astype(f32)
            value = part[0:8] + part[8:16] + part[16:24]
            for half in range(2):
                p = T // 128 + (by * 3 + bx) * 2 + half
                for c in range(3):
                    at = c * 24 + p
                    places[at : at + 1, :] = value[half * 4 + c : half * 4 + c + 1]

    def lane_block(b, carry):
        lanes = pl.ds(pl.multiple_of(b * 128, 128), 128)
        for g in range(K // 8):
            index = slots[pl.ds(pl.multiple_of(b * K + g * 8, 8), 8), :]
            low, high = index & 127, index >> 7
            total = jnp.zeros((8, 128), f32)
            value = [jnp.zeros((8, 128), f32) for _ in range(3)]
            for p in range(PIECES):
                here = high == p
                for c in range(3):
                    source = places[pl.ds(c * 24 + p, 8, stride=0), :]
                    value[c] = jnp.where(here, jnp.take_along_axis(source, low, axis=1), value[c])
            for c in range(3):
                apart = value[c] - frac[c : c + 1, lanes]
                apart = apart - jnp.floor(apart + 0.5)
                sine = sin_pi(apart)
                total = total + sine * sine
            chord[pl.ds(pl.multiple_of(b * K + g * 8, 8), 8), :] = total
        return carry

    lax.fori_loop(0, T // 128, lane_block, 0)


def add_messages(table, slots, filters, total, block, group):
    first = block * (K * 128) + group * 512
    ahead = [slots.at[pl.ds(c, K * T - 512)] for c in range(512)]
    for g in range(8):
        at = pl.ds(pl.multiple_of(block * 128 + g * 16, 16), 16)
        acc = total[at, :]
        parts = [acc[:8], acc[8:]]
        for j in range(4):
            weight = filters[j // 2, at, (j % 2) * C : (j % 2 + 1) * C].astype(f32)
            for n in range(2):
                c = j * 128 + g * 16 + n * 8
                source = pick8(table, lambda s: ahead[c + s][first])
                parts[n] = parts[n] + source * weight[n * 8 : n * 8 + 8]
        total[at, :] = jnp.concatenate(parts, axis=0)


def layer_kernel(
    slots_s, send, slots, frac, x_low, x_own, x_high, projected, state,
    w1, w2, w_update1, w_update2, w_in,
    state_out, proj_out, send_out, chord_out,
    table, places, wide1, wide2, filters, total, proj_table,
):
    rows_in = (x_low, x_own, x_high)
    fill_table(table, projected, rows_in, PACK)
    fill_filter_weights(w1, w2, 0, wide1, wide2)
    chords(slots, frac, rows_in, chord_out, places)
    total[...] = jnp.zeros_like(total)

    def make(group, carry):
        make_filters(chord_out, group, wide1, wide2, filters.at[group])
        return carry

    def use(i, carry):
        add_messages(table, slots_s, filters.at[i // 4], total, i % 4, i // 4)
        return carry

    lax.fori_loop(0, 8, make, 0)
    lax.fori_loop(0, 32, use, 0)
    new_state = update_tail(total, state, w_update1, w_update2, 0)
    state_out[...] = new_state
    projected1 = dot(new_state, w_in[1]).astype(bf16)
    proj_out[...] = projected1
    proj_table[...] = projected1.astype(f32)
    pick_send_rows(proj_table, send, send_out)


def filter_kernel(chord, w1, w2, out, wide1, wide2):
    step = pl.program_id(0)

    @pl.when(step == 0)
    def _():
        fill_filter_weights(w1, w2, 1, wide1, wide2)

    def make(i, carry):
        make_filters(chord, step * 2 + i, wide1, wide2, out.at[i])
        return carry

    lax.fori_loop(0, 2, make, 0)


def last_layer_kernel(
    slots_s, core, filters, x_low, x_own, x_high, projected, state,
    w_update1, w_update2, w_charge, phase, axis, digits,
    state_out, keep_out, give_out,
    table, total, left, sums,
):
    step = pl.program_id(0)

    @pl.when(step == 0)
    def _():
        fill_table(table, projected, (x_low, x_own, x_high), H)
        total[...] = jnp.zeros_like(total)

    def use(i, carry):
        add_messages(table, slots_s, filters.at[i // 4], total, i % 4, step * 2 + i // 4)
        return carry

    lax.fori_loop(0, 8, use, 0)

    @pl.when(step == 3)
    def _():
        new_state = update_tail(total, state, w_update1, w_update2, 1)
        state_out[...] = new_state
        charges = dot(w_charge[...], new_state, ((1,), (1,))).astype(bf16).astype(f32)
        for n in range(KX):
            left[n * Q : (n + 1) * Q, :T] = (charges * axis[n : n + 1, :]).astype(bf16)
            left[n * Q : (n + 1) * Q, T:] = (charges * axis[8 + n : 9 + n, :]).astype(bf16)
        sums[...] = jnp.zeros_like(sums)
        sums[:ROWS, : 2 * BETA] = dot(left[...], phase[...], ((1,), (1,)))
        sums[ROWS:, :] = digits[...]
        mine = pl.multiple_of(core[0] * HALF, HALF)
        keep_out[...] = sums[pl.ds(mine, HALF), :].astype(bf16)
        give_out[...] = sums[pl.ds(pl.multiple_of(HALF - mine, HALF), HALF), :].astype(bf16)


def field_kernel(
    core, own_half, other_half, phase, axis, screening, state, w_head, w_potential, w_energy,
    potentials_out, energies_out, response, sums,
):
    mine = pl.multiple_of(core[0] * HALF, HALF)
    sums[pl.ds(mine, HALF), :] = own_half[...].astype(f32)
    sums[pl.ds(pl.multiple_of(HALF - mine, HALF), HALF), :] = other_half[...].astype(f32)
    lane = rows_of((1, SUM_LANES), 1)
    beta = jnp.where(lane >= BETA, lane - BETA, lane)
    y = (beta * 79) >> 10
    ky = y - 6
    kz = beta - y * YZ - 6
    plane_sq = (ky * ky + kz * kz).astype(f32)
    digits = sums[ROWS:, :]
    packed = digits[0:8] + 3.0 * digits[8:16]
    ahead = pltpu.roll(packed, SUM_LANES - BETA, 1)
    behind = pltpu.roll(packed, BETA, 1)
    lane8 = rows_of((8, SUM_LANES), 1)
    count = jnp.where(lane8 < BETA, packed + 9.0 * ahead, behind + 9.0 * packed)
    square = rows_of((Q, Q), 0) == rows_of((Q, Q), 1)
    screen = jnp.sum(jnp.where(square, jnp.broadcast_to(screening[...], (Q, Q)), 0.0), axis=1, keepdims=True)
    for n in range(KX):
        norm_sq = plane_sq + float(n * n)
        kernel = jnp.exp(norm_sq * (-1.0 / 64.0)) * count[n : n + 1, :] / (norm_sq + screen)
        value = kernel * sums[n * Q : (n + 1) * Q, :]
        response[n * Q : (n + 1) * Q, :] = value[:, : 2 * BETA].astype(bf16)
    field = dot(response[...], phase[...])
    total = jnp.zeros((Q, T), f32)
    for n in range(KX):
        part = field[n * Q : (n + 1) * Q]
        total = total + part[:, :T] * axis[n : n + 1, :] + part[:, T:] * axis[8 + n : 9 + n, :]
    potentials = total * (4.0 / 256.0)
    potentials_out[...] = potentials
    summed = dot(state[...], w_head[...]) + dot(potentials.astype(bf16), w_potential[...], ((0,), (0,)))
    readout = silu(summed).astype(bf16)
    energies_out[...] = dot(w_energy[...], readout, ((1,), (1,)))


VMEM = pl.BlockSpec(memory_space=pltpu.VMEM)
SMEM = pl.BlockSpec(memory_space=pltpu.SMEM)


def shape(*dims, dtype=f32):
    return jax.ShapeDtypeStruct(dims, dtype)


def call(kernel, ins, outs, scratch, flops, moved):
    return pl.pallas_call(
        kernel,
        out_shape=outs,
        in_specs=ins,
        out_specs=jax.tree.map(lambda _: VMEM, outs),
        scratch_shapes=scratch,
        cost_estimate=pl.CostEstimate(flops=flops, bytes_accessed=moved, transcendentals=0),
    )


def halo(block):
    for axis in ("gx", "yz"):
        count = lax.axis_size(axis)
        forward = [(i, (i + 1) % count) for i in range(count)]
        backward = [(target, source) for source, target in forward]
        low = lax.ppermute(block, axis, forward)
        high = lax.ppermute(block, axis, backward)
        if axis == "gx":
            block = jnp.concatenate([low, block, high], axis=0)
    return low, block, high


RINGS = ((2, 16, 18), (4, 8, 12), (32, 64, 96))


def exchange(part, offset):
    count = lax.axis_size("gx") * lax.axis_size("yz")
    return lax.ppermute(part, ("gx", "yz"), [(i, i ^ offset) for i in range(count)])


def sum_everywhere(keep, give):
    part = (keep.astype(f32) + exchange(give, 1).astype(f32)).astype(bf16)
    for offsets in RINGS:
        taken = [exchange(part, o) for o in offsets]
        total = part.astype(f32)
        for one in taken:
            total = total + one.astype(f32)
        part = total.astype(bf16)
    return part, exchange(part, 1)


def shards(
    features, frac, neighbours, nbr_mask, send_list, wavevectors, w_in, w_filter1, w_filter2,
    w_update1, w_update2, w_charge, screening, w_head, w_potential, w_energy,
):
    projected, sent = call(
        first_kernel, [SMEM, VMEM, VMEM, VMEM, VMEM],
        (shape(T, C, dtype=bf16), shape(PACK, C, dtype=bf16)),
        [pltpu.VMEM((T, C), f32), pltpu.VMEM((32, 128), f32)], 20_000_000, 300_000,
    )(send_list, send_list.reshape(2, 128), features, frac, w_in)
    slots, phase, axis, digits = call(
        prepare_kernel, [VMEM] * 4,
        (shape(4 * K, 128, dtype=i32), shape(2 * BETA, 2 * T, dtype=bf16), shape(16, T), shape(16, SUM_LANES)),
        [pltpu.VMEM((2, BETA, T), f32)], 2_000_000_000, 4_000_000,
    )(neighbours, nbr_mask, frac, wavevectors)
    x_low, x_own, x_high = halo(sent)
    state, projected, sent, chord = call(
        layer_kernel, [SMEM, SMEM] + [VMEM] * 12,
        (shape(T, C, dtype=bf16), shape(T, C, dtype=bf16), shape(H, C, dtype=bf16), shape(4 * K, 128)),
        [
            pltpu.VMEM((SLOTS + 8, C), f32), pltpu.VMEM((72, 128), f32),
            pltpu.VMEM((4 * NR, 4 * C), bf16), pltpu.VMEM((2 * C, 2 * C), bf16),
            pltpu.VMEM((8, 2, T, 2 * C), bf16),
            pltpu.VMEM((T, C), f32), pltpu.VMEM((T, C), f32),
        ], 4_000_000_000, 4_000_000,
    )(
        slots.reshape(-1), send_list, slots, frac, x_low, x_own, x_high, projected, features,
        w_filter1, w_filter2, w_update1, w_update2, w_in,
    )
    x_low, x_own, x_high = halo(sent)
    whole = lambda a: pl.BlockSpec(a.shape, lambda i: (0,) * a.ndim)
    block = pl.BlockSpec((2, 2, T, 2 * C), lambda i: (i, 0, 0, 0))
    filters = pl.pallas_call(
        filter_kernel, grid=(4,),
        out_shape=shape(8, 2, T, 2 * C, dtype=bf16),
        in_specs=[whole(chord), whole(w_filter1), whole(w_filter2)], out_specs=block,
        scratch_shapes=[pltpu.VMEM((4 * NR, 4 * C), bf16), pltpu.VMEM((2 * C, 2 * C), bf16)],
        cost_estimate=pl.CostEstimate(flops=4_000_000_000, bytes_accessed=8_000_000, transcendentals=0),
    )(chord, w_filter1, w_filter2)
    rest = (x_low, x_own, x_high, projected, state, w_update1, w_update2, w_charge.T, phase, axis, digits)
    half = shape(HALF, SUM_LANES, dtype=bf16)
    half_spec = pl.BlockSpec(half.shape, lambda i: (0, 0))
    core = (lax.axis_index("yz") & 1).reshape(1)
    embeddings, keep, give = pl.pallas_call(
        last_layer_kernel, grid=(4,),
        out_shape=(shape(T, C, dtype=bf16), half, half),
        in_specs=[SMEM, SMEM, block] + [whole(a) for a in rest],
        out_specs=(pl.BlockSpec((T, C), lambda i: (0, 0)), half_spec, half_spec),
        scratch_shapes=[
            pltpu.VMEM((SLOTS + 8, C), f32), pltpu.VMEM((T, C), f32), pltpu.VMEM((ROWS, 2 * T), bf16),
            pltpu.VMEM((SUM_ROWS, SUM_LANES), f32),
        ],
        cost_estimate=pl.CostEstimate(flops=1_000_000_000, bytes_accessed=8_000_000, transcendentals=0),
    )(slots.reshape(-1), core, filters, *rest)
    own_half, other_half = sum_everywhere(keep, give)
    potentials, energies = call(
        field_kernel, [SMEM] + [VMEM] * 9, (shape(Q, T), shape(1, T)),
        [pltpu.VMEM((ROWS, 2 * BETA), bf16), pltpu.VMEM((SUM_ROWS, SUM_LANES), f32)], 100_000_000, 2_000_000,
    )(
        core, own_half, other_half, phase, axis, screening.reshape(1, Q), embeddings, w_head, w_potential,
        w_energy.reshape(1, C),
    )
    return embeddings, potentials, energies.reshape(T)


def solution(mesh):
    atoms = ("gx", "yz")
    return jax.shard_map(
        shards,
        mesh=mesh,
        in_specs=(P(atoms, None), P(None, atoms), P(None, atoms), P(None, atoms), P(atoms), P(None, atoms))
        + (P(),) * 10,
        out_specs=(P(atoms, None), P(None, atoms), P(atoms)),
        check_vma=False,
    )
```

```python
import functools
import math

import jax
import jax.numpy as jnp
from jax import lax
from jax.experimental import pallas as pl
from jax.experimental.pallas import tpu as pltpu
from jax.sharding import PartitionSpec as P

C = 128
NR = 32
Q = 16
K = 32
SIDE = 16
T = 512
H = 256
PACK = H + 32
SLOTS = T + 9 * H
ZERO = SLOTS
PIECES = SLOTS // 128
KX = 7
YZ = 13
BETA = 176
ROWS = KX * Q
SUM_ROWS = ROWS + 16
SUM_LANES = 384
HALF = SUM_ROWS // 2
f32, bf16, i32 = jnp.float32, jnp.bfloat16, jnp.int32


def rows_of(shape, dim):
    return lax.broadcasted_iota(i32, shape, dim)


def dot(a, b, dims=((1,), (0,))):
    return lax.dot_general(a, b, (dims, ((), ())), preferred_element_type=f32)


def silu(v):
    half = 0.5 * v
    return half + half * jnp.tanh(half)


def sin_pi(x):
    y = x * x
    total = jnp.full_like(x, math.pi**13 / math.factorial(13))
    for order in (11, 9, 7, 5, 3, 1):
        sign = -1.0 if order % 4 == 3 else 1.0
        total = total * y + sign * math.pi**order / math.factorial(order)
    return total * x


def pick8(table, index_of):
    sub = rows_of((8, C), 0)
    picked = table[pl.ds(index_of(0), 8, stride=0), :]
    for j in range(1, 8):
        picked = jnp.where(sub == j, table[pl.ds(index_of(j), 8, stride=0), :], picked)
    return picked


def pick_send_rows(table, send, out):
    def group(g, carry):
        base = g * 16
        low = pick8(table, lambda j: send[base + j])
        high = pick8(table, lambda j: send[base + 8 + j])
        out[pl.ds(pl.multiple_of(base, 16), 16), :] = jnp.concatenate([low, high], axis=0).astype(bf16)
        return carry

    lax.fori_loop(0, H // 16, group, 0)


def first_kernel(send, send_lanes, features, frac, w_in, proj_out, out, table, parts):
    projected = dot(features[...], w_in[0]).astype(bf16)
    proj_out[...] = projected
    table[...] = projected.astype(f32)
    pick_send_rows(table, send, out)
    parts[...] = jnp.zeros_like(parts)
    for half in range(2):
        index = jnp.broadcast_to(send_lanes[half : half + 1, :], (8, 128))
        low, high = index & 127, index >> 7
        for c in range(3):
            value = jnp.zeros((8, 128), f32)
            for p in range(T // 128):
                source = jnp.broadcast_to(frac[c : c + 1, p * 128 : (p + 1) * 128], (8, 128))
                value = jnp.where(high == p, jnp.take_along_axis(source, low, axis=1), value)
            value = value[0:1]
            for part in range(3):
                rounded = value.astype(bf16).astype(f32)
                row = part * 8 + half * 4 + c
                parts[row : row + 1, :] = rounded
                value = value - rounded
    out[H:PACK, :] = parts[...].astype(bf16)


def prepare_kernel(neighbours, mask, frac, waves, slots_out, phase_out, axis_out, digits_out, plane):
    u = neighbours[...] - T
    row = (u * 43691) >> 21
    col = u - row * 48
    block = (col >> 4) * 3 + (row >> 4)
    moved = T + block * H + (row & 15) * SIDE + (col & 15)
    slots = jnp.where(mask[...] != 0, jnp.where(u < 0, u + T, moved), ZERO)
    for b in range(T // 128):
        slots_out[b * K : (b + 1) * K, :] = slots[:, b * 128 : (b + 1) * 128]

    def turn(c):
        harmonics = []
        for n in range(KX):
            x = frac[c : c + 1, :] * float(n)
            x = x - jnp.floor(x + 0.5)
            s = sin_pi(jnp.clip(2.0 * x - jnp.floor(2.0 * x + 0.5), -0.5, 0.5))
            odd = (jnp.floor(2.0 * x + 0.5).astype(i32) & 1) != 0
            sine = jnp.where(odd, -s, s)
            y = 2.0 * x + 0.5
            t = y - jnp.floor(y + 0.5)
            s2 = sin_pi(jnp.clip(t, -0.5, 0.5))
            odd2 = (jnp.floor(y + 0.5).astype(i32) & 1) != 0
            cosine = jnp.where(odd2, -s2, s2)
            harmonics.append((cosine, sine))
        return harmonics

    hx, hy, hz = turn(0), turn(1), turn(2)
    axis_out[...] = jnp.zeros_like(axis_out)
    for n in range(KX):
        axis_out[n : n + 1, :] = hx[n][0]
        axis_out[8 + n : 9 + n, :] = hx[n][1]

    def signed(h, k):
        c, s = h[abs(k)]
        return (c, s) if k >= 0 else (c, -s)

    zc = jnp.concatenate([signed(hz, k)[0] for k in range(-6, 7)], axis=0)
    zs = jnp.concatenate([signed(hz, k)[1] for k in range(-6, 7)], axis=0)
    plane[...] = jnp.zeros_like(plane)
    for n in range(YZ):
        yc, ys = signed(hy, n - 6)
        c = yc * zc - ys * zs
        s = ys * zc + yc * zs
        plane[0, n * YZ : (n + 1) * YZ, :] = c
        plane[1, n * YZ : (n + 1) * YZ, :] = s
    phase_out[:BETA, :T] = plane[0].astype(bf16)
    phase_out[:BETA, T:] = (-plane[1]).astype(bf16)
    phase_out[BETA:, :T] = plane[1].astype(bf16)
    phase_out[BETA:, T:] = plane[0].astype(bf16)

    modes = waves.shape[1]
    flip = jnp.where(waves[0:1, :] < 0, -1, 1)
    kx = waves[0:1, :] * flip
    beta = (waves[1:2, :] * flip + 6) * YZ + waves[2:3, :] * flip + 6
    hot_x = (rows_of((8, modes), 0) == kx).astype(f32).astype(bf16)
    r = rows_of((SUM_LANES, modes), 0)
    r = jnp.where(r >= BETA, r - BETA, r)
    hot_b = (r == beta).astype(f32).astype(bf16)
    count = dot(hot_x, hot_b, ((1,), (1,))).astype(i32)
    thirds = [count]
    for _ in range(3):
        thirds.append((thirds[-1] * 171) >> 9)
    digit = [a - 3 * b for a, b in zip(thirds[:3], thirds[1:])] + [thirds[3]]
    lane = rows_of((8, SUM_LANES), 1)
    first = lane < BETA
    keep = lane < 2 * BETA
    low = jnp.where(first, digit[0], digit[2])
    high = jnp.where(first, digit[1], digit[3])
    digits_out[0:8, :] = jnp.where(keep, low, 0).astype(f32)
    digits_out[8:16, :] = jnp.where(keep, high, 0).astype(f32)


def fill_table(table, projected, rows_in, stride):
    table[0:T, :] = projected[...].astype(f32)
    for by in range(3):
        for bx in range(3):
            at = T + (by * 3 + bx) * H
            table[at : at + H, :] = rows_in[by][bx * stride : bx * stride + H, :].astype(f32)
    table[ZERO : ZERO + 8, :] = jnp.zeros((8, C), f32)


def fill_filter_weights(w1, w2, layer, wide1, wide2):
    wide1[...] = jnp.zeros_like(wide1)
    wide2[...] = jnp.zeros_like(wide2)
    for j in range(4):
        wide1[j * NR : (j + 1) * NR, j * C : (j + 1) * C] = w1[layer]
    for j in range(2):
        wide2[j * C : (j + 1) * C, j * C : (j + 1) * C] = w2[layer]


def radial_of(chord):
    scaled = chord * (31.0 / 3.0) - rows_of((NR, 128), 0).astype(f32)
    return jnp.exp(-0.5 * scaled * scaled).astype(bf16)


def make_filters(chord, group, wide1, wide2, out):
    radial = jnp.concatenate(
        [
            jnp.concatenate(
                [radial_of(chord[pl.ds(b * K + group * 4 + j, NR, stride=0), :]) for b in range(T // 128)], axis=1
            )
            for j in range(4)
        ],
        axis=0,
    )
    for h in range(2):
        hidden = silu(dot(radial, wide1[:, h * 2 * C : (h + 1) * 2 * C], ((0,), (0,)))).astype(bf16)
        out[h] = dot(hidden, wide2[...]).astype(bf16)


def update_tail(total, state, w_update1, w_update2, layer):
    aggregate = (total[...] * (1.0 / math.sqrt(K))).astype(bf16)
    update = silu(dot(aggregate, w_update1[layer])).astype(bf16)
    return (state[...].astype(f32) + dot(update, w_update2[layer])).astype(bf16)


def chords(slots, frac, rows_in, chord, places):
    for c in range(3):
        for p in range(T // 128):
            places[c * 24 + p : c * 24 + p + 1, :] = frac[c : c + 1, p * 128 : (p + 1) * 128]
    for by in range(3):
        for bx in range(3):
            part = rows_in[by][bx * PACK + H : (bx + 1) * PACK, :].astype(f32)
            value = part[0:8] + part[8:16] + part[16:24]
            for half in range(2):
                p = T // 128 + (by * 3 + bx) * 2 + half
                for c in range(3):
                    at = c * 24 + p
                    places[at : at + 1, :] = value[half * 4 + c : half * 4 + c + 1]

    def lane_block(b, carry):
        lanes = pl.ds(pl.multiple_of(b * 128, 128), 128)
        for g in range(K // 8):
            index = slots[pl.ds(pl.multiple_of(b * K + g * 8, 8), 8), :]
            low, high = index & 127, index >> 7
            total = jnp.zeros((8, 128), f32)
            value = [jnp.zeros((8, 128), f32) for _ in range(3)]
            for p in range(PIECES):
                here = high == p
                for c in range(3):
                    source = places[pl.ds(c * 24 + p, 8, stride=0), :]
                    value[c] = jnp.where(here, jnp.take_along_axis(source, low, axis=1), value[c])
            for c in range(3):
                apart = value[c] - frac[c : c + 1, lanes]
                apart = apart - jnp.floor(apart + 0.5)
                sine = sin_pi(apart)
                total = total + sine * sine
            chord[pl.ds(pl.multiple_of(b * K + g * 8, 8), 8), :] = total
        return carry

    lax.fori_loop(0, T // 128, lane_block, 0)


def add_messages(table, slots, filters, total, block, group):
    first = block * (K * 128) + group * 512
    ahead = [slots.at[pl.ds(c, K * T - 512)] for c in range(512)]
    for g in range(8):
        at = pl.ds(pl.multiple_of(block * 128 + g * 16, 16), 16)
        acc = total[at, :]
        parts = [acc[:8], acc[8:]]
        for j in range(4):
            weight = filters[j // 2, at, (j % 2) * C : (j % 2 + 1) * C].astype(f32)
            for n in range(2):
                c = j * 128 + g * 16 + n * 8
                source = pick8(table, lambda s: ahead[c + s][first])
                parts[n] = parts[n] + source * weight[n * 8 : n * 8 + 8]
        total[at, :] = jnp.concatenate(parts, axis=0)


def layer_kernel(
    slots_hbm, send, slots, frac, x_low, x_own, x_high, projected, state,
    w1, w2, w_update1, w_update2, w_in,
    state_out, proj_out, send_out, chord_out,
    table, places, wide1, wide2, filters, total, proj_table, slots_s, arrived,
):
    fetch = pltpu.make_async_copy(slots_hbm, slots_s, arrived)
    fetch.start()
    rows_in = (x_low, x_own, x_high)
    fill_table(table, projected, rows_in, PACK)
    fill_filter_weights(w1, w2, 0, wide1, wide2)
    chords(slots, frac, rows_in, chord_out, places)
    total[...] = jnp.zeros_like(total)

    def make(group, carry):
        make_filters(chord_out, group, wide1, wide2, filters.at[group])
        return carry

    def use(i, carry):
        add_messages(table, slots_s, filters.at[i // 4], total, i % 4, i // 4)
        return carry

    lax.fori_loop(0, 8, make, 0)
    fetch.wait()
    lax.fori_loop(0, 32, use, 0)
    new_state = update_tail(total, state, w_update1, w_update2, 0)
    state_out[...] = new_state
    projected1 = dot(new_state, w_in[1]).astype(bf16)
    proj_out[...] = projected1
    proj_table[...] = projected1.astype(f32)
    pick_send_rows(proj_table, send, send_out)


def filter_kernel(chord, w1, w2, out, wide1, wide2):
    step = pl.program_id(0)

    @pl.when(step == 0)
    def _():
        fill_filter_weights(w1, w2, 1, wide1, wide2)

    def make(i, carry):
        make_filters(chord, step * 2 + i, wide1, wide2, out.at[i])
        return carry

    lax.fori_loop(0, 2, make, 0)


def last_layer_kernel(
    slots_s, core, filters, x_low, x_own, x_high, projected, state,
    w_update1, w_update2, w_charge, phase, axis, digits,
    state_out, keep_out, give_out,
    table, total, left, sums,
):
    step = pl.program_id(0)

    @pl.when(step == 0)
    def _():
        fill_table(table, projected, (x_low, x_own, x_high), H)
        total[...] = jnp.zeros_like(total)

    def use(i, carry):
        add_messages(table, slots_s, filters.at[i // 4], total, i % 4, step * 2 + i // 4)
        return carry

    lax.fori_loop(0, 8, use, 0)

    @pl.when(step == 3)
    def _():
        new_state = update_tail(total, state, w_update1, w_update2, 1)
        state_out[...] = new_state
        charges = dot(w_charge[...], new_state, ((1,), (1,))).astype(bf16).astype(f32)
        for n in range(KX):
            left[n * Q : (n + 1) * Q, :T] = (charges * axis[n : n + 1, :]).astype(bf16)
            left[n * Q : (n + 1) * Q, T:] = (charges * axis[8 + n : 9 + n, :]).astype(bf16)
        sums[...] = jnp.zeros_like(sums)
        sums[:ROWS, : 2 * BETA] = dot(left[...], phase[...], ((1,), (1,)))
        sums[ROWS:, :] = digits[...]
        mine = pl.multiple_of(core[0] * HALF, HALF)
        keep_out[...] = sums[pl.ds(mine, HALF), :].astype(bf16)
        give_out[...] = sums[pl.ds(pl.multiple_of(HALF - mine, HALF), HALF), :].astype(bf16)


def field_kernel(
    core, own_half, other_half, phase, axis, screening, head, w_potential, w_energy,
    potentials_out, energies_out, response, sums,
):
    mine = pl.multiple_of(core[0] * HALF, HALF)
    sums[pl.ds(mine, HALF), :] = own_half[...].astype(f32)
    sums[pl.ds(pl.multiple_of(HALF - mine, HALF), HALF), :] = other_half[...].astype(f32)
    lane = rows_of((1, SUM_LANES), 1)
    beta = jnp.where(lane >= BETA, lane - BETA, lane)
    y = (beta * 79) >> 10
    ky = y - 6
    kz = beta - y * YZ - 6
    plane_sq = (ky * ky + kz * kz).astype(f32)
    digits = sums[ROWS:, :]
    packed = digits[0:8] + 3.0 * digits[8:16]
    ahead = pltpu.roll(packed, SUM_LANES - BETA, 1)
    behind = pltpu.roll(packed, BETA, 1)
    lane8 = rows_of((8, SUM_LANES), 1)
    count = jnp.where(lane8 < BETA, packed + 9.0 * ahead, behind + 9.0 * packed)
    square = rows_of((Q, Q), 0) == rows_of((Q, Q), 1)
    screen = jnp.sum(jnp.where(square, jnp.broadcast_to(screening[...], (Q, Q)), 0.0), axis=1, keepdims=True)
    for n in range(KX):
        norm_sq = plane_sq + float(n * n)
        kernel = jnp.exp(norm_sq * (-1.0 / 64.0)) * count[n : n + 1, :] / (norm_sq + screen)
        value = kernel * sums[n * Q : (n + 1) * Q, :]
        response[n * Q : (n + 1) * Q, :] = value[:, : 2 * BETA].astype(bf16)
    field = dot(response[...], phase[...])
    total = jnp.zeros((Q, T), f32)
    for n in range(KX):
        part = field[n * Q : (n + 1) * Q]
        total = total + part[:, :T] * axis[n : n + 1, :] + part[:, T:] * axis[8 + n : 9 + n, :]
    potentials = total * (4.0 / 256.0)
    potentials_out[...] = potentials
    summed = head[...] + dot(potentials.astype(bf16), w_potential[...], ((0,), (0,)))
    readout = silu(summed).astype(bf16)
    energies_out[...] = dot(w_energy[...], readout, ((1,), (1,)))


VMEM = pl.BlockSpec(memory_space=pltpu.VMEM)
SMEM = pl.BlockSpec(memory_space=pltpu.SMEM)


def shape(*dims, dtype=f32):
    return jax.ShapeDtypeStruct(dims, dtype)


def call(kernel, ins, outs, scratch, flops, moved):
    return pl.pallas_call(
        kernel,
        out_shape=outs,
        in_specs=ins,
        out_specs=jax.tree.map(lambda _: VMEM, outs),
        scratch_shapes=scratch,
        cost_estimate=pl.CostEstimate(flops=flops, bytes_accessed=moved, transcendentals=0),
    )


def near(x):
    return pltpu.with_memory_space_constraint(x, pltpu.VMEM)


def halo(block):
    for axis in ("gx", "yz"):
        count = lax.axis_size(axis)
        forward = [(i, (i + 1) % count) for i in range(count)]
        backward = [(target, source) for source, target in forward]
        low = lax.ppermute(block, axis, forward)
        high = lax.ppermute(block, axis, backward)
        if axis == "gx":
            block = jnp.concatenate([low, block, high], axis=0)
    return near(low), near(block), near(high)


RINGS = ((2, 16, 18), (4, 8, 12), (32, 64, 96))


def exchange(part, offset):
    count = lax.axis_size("gx") * lax.axis_size("yz")
    return lax.ppermute(part, ("gx", "yz"), [(i, i ^ offset) for i in range(count)])


def sum_everywhere(keep, give):
    part = (keep.astype(f32) + exchange(give, 1).astype(f32)).astype(bf16)
    for offsets in RINGS:
        taken = [exchange(part, o) for o in offsets]
        total = part.astype(f32)
        for one in taken:
            total = total + one.astype(f32)
        part = total.astype(bf16)
    return part, exchange(part, 1)


def shards(
    features, frac, neighbours, nbr_mask, send_list, wavevectors, w_in, w_filter1, w_filter2,
    w_update1, w_update2, w_charge, screening, w_head, w_potential, w_energy,
):
    projected, sent = call(
        first_kernel, [SMEM, VMEM, VMEM, VMEM, VMEM],
        (shape(T, C, dtype=bf16), shape(PACK, C, dtype=bf16)),
        [pltpu.VMEM((T, C), f32), pltpu.VMEM((32, 128), f32)], 20_000_000, 300_000,
    )(send_list, send_list.reshape(2, 128), features, frac, w_in)
    slots, phase, axis, digits = call(
        prepare_kernel, [VMEM] * 4,
        (shape(4 * K, 128, dtype=i32), shape(2 * BETA, 2 * T, dtype=bf16), shape(16, T), shape(16, SUM_LANES)),
        [pltpu.VMEM((2, BETA, T), f32)], 2_000_000_000, 4_000_000,
    )(neighbours, nbr_mask, frac, wavevectors)
    x_low, x_own, x_high = halo(sent)
    state, projected, sent, chord = call(
        layer_kernel, [pl.BlockSpec(memory_space=pl.ANY), SMEM] + [VMEM] * 12,
        (shape(T, C, dtype=bf16), shape(T, C, dtype=bf16), shape(H, C, dtype=bf16), shape(4 * K, 128)),
        [
            pltpu.VMEM((SLOTS + 8, C), f32), pltpu.VMEM((72, 128), f32),
            pltpu.VMEM((4 * NR, 4 * C), bf16), pltpu.VMEM((2 * C, 2 * C), bf16),
            pltpu.VMEM((8, 2, T, 2 * C), bf16),
            pltpu.VMEM((T, C), f32), pltpu.VMEM((T, C), f32),
            pltpu.SMEM((K * T,), i32), pltpu.SemaphoreType.DMA,
        ], 4_000_000_000, 4_000_000,
    )(
        slots.reshape(-1), send_list, slots, near(frac), x_low, x_own, x_high, near(projected), near(features),
        near(w_filter1), near(w_filter2), near(w_update1), near(w_update2), near(w_in),
    )
    x_low, x_own, x_high = halo(sent)
    whole = lambda a: pl.BlockSpec(a.shape, lambda i: (0,) * a.ndim)
    block = pl.BlockSpec((2, 2, T, 2 * C), lambda i: (i, 0, 0, 0))
    filters = pl.pallas_call(
        filter_kernel, grid=(4,),
        out_shape=shape(8, 2, T, 2 * C, dtype=bf16),
        in_specs=[whole(chord), whole(w_filter1), whole(w_filter2)], out_specs=block,
        scratch_shapes=[pltpu.VMEM((4 * NR, 4 * C), bf16), pltpu.VMEM((2 * C, 2 * C), bf16)],
        cost_estimate=pl.CostEstimate(flops=4_000_000_000, bytes_accessed=8_000_000, transcendentals=0),
    )(chord, w_filter1, w_filter2)
    phase, axis = near(phase), near(axis)
    rest = (x_low, x_own, x_high, near(projected), near(state), near(w_update1), near(w_update2))
    rest = rest + (near(w_charge.T), phase, axis, near(digits))
    half = shape(HALF, SUM_LANES, dtype=bf16)
    half_spec = pl.BlockSpec(half.shape, lambda i: (0, 0))
    core = (lax.axis_index("yz") & 1).reshape(1)
    embeddings, keep, give = pl.pallas_call(
        last_layer_kernel, grid=(4,),
        out_shape=(shape(T, C, dtype=bf16), half, half),
        in_specs=[SMEM, SMEM, block] + [whole(a) for a in rest],
        out_specs=(pl.BlockSpec((T, C), lambda i: (0, 0)), half_spec, half_spec),
        scratch_shapes=[
            pltpu.VMEM((SLOTS + 8, C), f32), pltpu.VMEM((T, C), f32), pltpu.VMEM((ROWS, 2 * T), bf16),
            pltpu.VMEM((SUM_ROWS, SUM_LANES), f32),
        ],
        cost_estimate=pl.CostEstimate(flops=1_000_000_000, bytes_accessed=8_000_000, transcendentals=0),
    )(slots.reshape(-1), core, filters, *rest)
    own_half, other_half = sum_everywhere(keep, give)
    head = dot(embeddings, w_head)
    potentials, energies = call(
        field_kernel, [SMEM] + [VMEM] * 8, (shape(Q, T), shape(1, T)),
        [pltpu.VMEM((ROWS, 2 * BETA), bf16), pltpu.VMEM((SUM_ROWS, SUM_LANES), f32)], 100_000_000, 2_000_000,
    )(
        core, near(own_half), near(other_half), phase, axis, near(screening.reshape(1, Q)), near(head),
        near(w_potential), near(w_energy.reshape(1, C)),
    )
    return embeddings, potentials, energies.reshape(T)


def solution(mesh):
    atoms = ("gx", "yz")
    return jax.shard_map(
        shards,
        mesh=mesh,
        in_specs=(P(atoms, None), P(None, atoms), P(None, atoms), P(None, atoms), P(atoms), P(None, atoms))
        + (P(),) * 10,
        out_specs=(P(atoms, None), P(None, atoms), P(atoms)),
        check_vma=False,
    )
```

```python
import functools
import math

import jax
import jax.numpy as jnp
from jax import lax
from jax.experimental import pallas as pl
from jax.experimental.pallas import tpu as pltpu
from jax.sharding import PartitionSpec as P

C = 128
NR = 32
Q = 16
K = 32
SIDE = 16
T = 512
H = 256
PACK = H + 32
SLOTS = T + 9 * H
ZERO = SLOTS
PIECES = SLOTS // 128
KX = 7
YZ = 13
BETA = 176
ROWS = KX * Q
SUM_ROWS = ROWS + 16
SUM_LANES = 384
HALF = SUM_ROWS // 2
f32, bf16, i32 = jnp.float32, jnp.bfloat16, jnp.int32


def rows_of(shape, dim):
    return lax.broadcasted_iota(i32, shape, dim)


def dot(a, b, dims=((1,), (0,))):
    return lax.dot_general(a, b, (dims, ((), ())), preferred_element_type=f32)


def silu(v):
    half = 0.5 * v
    return half + half * jnp.tanh(half)


def sin_pi(x):
    y = x * x
    total = jnp.full_like(x, math.pi**13 / math.factorial(13))
    for order in (11, 9, 7, 5, 3, 1):
        sign = -1.0 if order % 4 == 3 else 1.0
        total = total * y + sign * math.pi**order / math.factorial(order)
    return total * x


def pick8(table, index_of):
    sub = rows_of((8, C), 0)
    picked = table[pl.ds(index_of(0), 8, stride=0), :]
    for j in range(1, 8):
        picked = jnp.where(sub == j, table[pl.ds(index_of(j), 8, stride=0), :], picked)
    return picked


def pick_send_rows(table, send, out):
    def group(g, carry):
        base = g * 16
        low = pick8(table, lambda j: send[base + j])
        high = pick8(table, lambda j: send[base + 8 + j])
        out[pl.ds(pl.multiple_of(base, 16), 16), :] = jnp.concatenate([low, high], axis=0).astype(bf16)
        return carry

    lax.fori_loop(0, H // 16, group, 0)


def first_kernel(send, send_lanes, features, frac, w_in, proj_out, out, table, parts):
    projected = dot(features[...], w_in[0]).astype(bf16)
    proj_out[...] = projected
    table[...] = projected.astype(f32)
    pick_send_rows(table, send, out)
    parts[...] = jnp.zeros_like(parts)
    for half in range(2):
        index = jnp.broadcast_to(send_lanes[half : half + 1, :], (8, 128))
        low, high = index & 127, index >> 7
        for c in range(3):
            value = jnp.zeros((8, 128), f32)
            for p in range(T // 128):
                source = jnp.broadcast_to(frac[c : c + 1, p * 128 : (p + 1) * 128], (8, 128))
                value = jnp.where(high == p, jnp.take_along_axis(source, low, axis=1), value)
            value = value[0:1]
            for part in range(3):
                rounded = value.astype(bf16).astype(f32)
                row = part * 8 + half * 4 + c
                parts[row : row + 1, :] = rounded
                value = value - rounded
    out[H:PACK, :] = parts[...].astype(bf16)


def prepare_kernel(neighbours, mask, frac, waves, slots_out, phase_out, axis_out, digits_out, plane):
    u = neighbours[...] - T
    row = (u * 43691) >> 21
    col = u - row * 48
    block = (col >> 4) * 3 + (row >> 4)
    moved = T + block * H + (row & 15) * SIDE + (col & 15)
    slots = jnp.where(mask[...] != 0, jnp.where(u < 0, u + T, moved), ZERO)
    for b in range(T // 128):
        slots_out[b * K : (b + 1) * K, :] = slots[:, b * 128 : (b + 1) * 128]

    def turn(c):
        harmonics = []
        for n in range(KX):
            x = frac[c : c + 1, :] * float(n)
            x = x - jnp.floor(x + 0.5)
            s = sin_pi(jnp.clip(2.0 * x - jnp.floor(2.0 * x + 0.5), -0.5, 0.5))
            odd = (jnp.floor(2.0 * x + 0.5).astype(i32) & 1) != 0
            sine = jnp.where(odd, -s, s)
            y = 2.0 * x + 0.5
            t = y - jnp.floor(y + 0.5)
            s2 = sin_pi(jnp.clip(t, -0.5, 0.5))
            odd2 = (jnp.floor(y + 0.5).astype(i32) & 1) != 0
            cosine = jnp.where(odd2, -s2, s2)
            harmonics.append((cosine, sine))
        return harmonics

    hx, hy, hz = turn(0), turn(1), turn(2)
    axis_out[...] = jnp.zeros_like(axis_out)
    for n in range(KX):
        axis_out[n : n + 1, :] = hx[n][0]
        axis_out[8 + n : 9 + n, :] = hx[n][1]

    def signed(h, k):
        c, s = h[abs(k)]
        return (c, s) if k >= 0 else (c, -s)

    zc = jnp.concatenate([signed(hz, k)[0] for k in range(-6, 7)], axis=0)
    zs = jnp.concatenate([signed(hz, k)[1] for k in range(-6, 7)], axis=0)
    plane[...] = jnp.zeros_like(plane)
    for n in range(YZ):
        yc, ys = signed(hy, n - 6)
        c = yc * zc - ys * zs
        s = ys * zc + yc * zs
        plane[0, n * YZ : (n + 1) * YZ, :] = c
        plane[1, n * YZ : (n + 1) * YZ, :] = s
    phase_out[:BETA, :T] = plane[0].astype(bf16)
    phase_out[:BETA, T:] = (-plane[1]).astype(bf16)
    phase_out[BETA:, :T] = plane[1].astype(bf16)
    phase_out[BETA:, T:] = plane[0].astype(bf16)

    modes = waves.shape[1]
    flip = jnp.where(waves[0:1, :] < 0, -1, 1)
    kx = waves[0:1, :] * flip
    beta = (waves[1:2, :] * flip + 6) * YZ + waves[2:3, :] * flip + 6
    hot_x = (rows_of((8, modes), 0) == kx).astype(f32).astype(bf16)
    r = rows_of((SUM_LANES, modes), 0)
    r = jnp.where(r >= BETA, r - BETA, r)
    hot_b = (r == beta).astype(f32).astype(bf16)
    count = dot(hot_x, hot_b, ((1,), (1,))).astype(i32)
    thirds = [count]
    for _ in range(3):
        thirds.append((thirds[-1] * 171) >> 9)
    digit = [a - 3 * b for a, b in zip(thirds[:3], thirds[1:])] + [thirds[3]]
    lane = rows_of((8, SUM_LANES), 1)
    first = lane < BETA
    keep = lane < 2 * BETA
    low = jnp.where(first, digit[0], digit[2])
    high = jnp.where(first, digit[1], digit[3])
    digits_out[0:8, :] = jnp.where(keep, low, 0).astype(f32)
    digits_out[8:16, :] = jnp.where(keep, high, 0).astype(f32)


def fill_table(table, projected, rows_in, stride):
    table[0:T, :] = projected[...].astype(f32)
    for by in range(3):
        for bx in range(3):
            at = T + (by * 3 + bx) * H
            table[at : at + H, :] = rows_in[by][bx * stride : bx * stride + H, :].astype(f32)
    table[ZERO : ZERO + 8, :] = jnp.zeros((8, C), f32)


def fill_filter_weights(w1, w2, layer, wide1, wide2):
    wide1[...] = jnp.zeros_like(wide1)
    wide2[...] = jnp.zeros_like(wide2)
    for j in range(4):
        wide1[j * NR : (j + 1) * NR, j * C : (j + 1) * C] = w1[layer]
    for j in range(2):
        wide2[j * C : (j + 1) * C, j * C : (j + 1) * C] = w2[layer]


def radial_of(chord):
    scaled = chord * (31.0 / 3.0) - rows_of((NR, 128), 0).astype(f32)
    return jnp.exp(-0.5 * scaled * scaled).astype(bf16)


def make_filters(chord, group, wide1, wide2, out):
    radial = jnp.concatenate(
        [
            jnp.concatenate(
                [radial_of(chord[pl.ds(b * K + group * 4 + j, NR, stride=0), :]) for b in range(T // 128)], axis=1
            )
            for j in range(4)
        ],
        axis=0,
    )
    for h in range(2):
        hidden = silu(dot(radial, wide1[:, h * 2 * C : (h + 1) * 2 * C], ((0,), (0,)))).astype(bf16)
        out[h] = dot(hidden, wide2[...]).astype(bf16)


def update_tail(total, state, w_update1, w_update2, layer):
    aggregate = (total[...] * (1.0 / math.sqrt(K))).astype(bf16)
    update = silu(dot(aggregate, w_update1[layer])).astype(bf16)
    return (state[...].astype(f32) + dot(update, w_update2[layer])).astype(bf16)


def chords(slots, frac, rows_in, chord, places):
    for c in range(3):
        for p in range(T // 128):
            places[c * 24 + p : c * 24 + p + 1, :] = frac[c : c + 1, p * 128 : (p + 1) * 128]
    for by in range(3):
        for bx in range(3):
            part = rows_in[by][bx * PACK + H : (bx + 1) * PACK, :].astype(f32)
            value = part[0:8] + part[8:16] + part[16:24]
            for half in range(2):
                p = T // 128 + (by * 3 + bx) * 2 + half
                for c in range(3):
                    at = c * 24 + p
                    places[at : at + 1, :] = value[half * 4 + c : half * 4 + c + 1]

    def lane_block(b, carry):
        lanes = pl.ds(pl.multiple_of(b * 128, 128), 128)
        for g in range(K // 8):
            index = slots[pl.ds(pl.multiple_of(b * K + g * 8, 8), 8), :]
            low, high = index & 127, index >> 7
            total = jnp.zeros((8, 128), f32)
            value = [jnp.zeros((8, 128), f32) for _ in range(3)]
            for p in range(PIECES):
                here = high == p
                for c in range(3):
                    source = places[pl.ds(c * 24 + p, 8, stride=0), :]
                    value[c] = jnp.where(here, jnp.take_along_axis(source, low, axis=1), value[c])
            for c in range(3):
                apart = value[c] - frac[c : c + 1, lanes]
                apart = apart - jnp.floor(apart + 0.5)
                sine = sin_pi(apart)
                total = total + sine * sine
            chord[pl.ds(pl.multiple_of(b * K + g * 8, 8), 8), :] = total
        return carry

    lax.fori_loop(0, T // 128, lane_block, 0)


def add_messages(table, slots, filters, total, block, group):
    first = block * (K * 128) + group * 512
    ahead = [slots.at[pl.ds(c, K * T - 512)] for c in range(512)]
    for g in range(8):
        at = pl.ds(pl.multiple_of(block * 128 + g * 16, 16), 16)
        acc = total[at, :]
        parts = [acc[:8], acc[8:]]
        for j in range(4):
            weight = filters[j // 2, at, (j % 2) * C : (j % 2 + 1) * C].astype(f32)
            for n in range(2):
                c = j * 128 + g * 16 + n * 8
                source = pick8(table, lambda s: ahead[c + s][first])
                parts[n] = parts[n] + source * weight[n * 8 : n * 8 + 8]
        total[at, :] = jnp.concatenate(parts, axis=0)


def layer_kernel(
    slots_hbm, send, slots, frac, x_low, x_own, x_high, projected, state,
    w1, w2, w_update1, w_update2, w_in,
    state_out, proj_out, send_out, chord_out,
    table, places, wide1, wide2, filters, total, proj_table, slots_s, arrived,
):
    fetch = pltpu.make_async_copy(slots_hbm, slots_s, arrived)
    fetch.start()
    rows_in = (x_low, x_own, x_high)
    fill_table(table, projected, rows_in, PACK)
    fill_filter_weights(w1, w2, 0, wide1, wide2)
    chords(slots, frac, rows_in, chord_out, places)
    total[...] = jnp.zeros_like(total)

    def make(group, carry):
        make_filters(chord_out, group, wide1, wide2, filters.at[group])
        return carry

    def use(i, carry):
        add_messages(table, slots_s, filters.at[i // 4], total, i % 4, i // 4)
        return carry

    lax.fori_loop(0, 8, make, 0)
    fetch.wait()
    lax.fori_loop(0, 32, use, 0)
    new_state = update_tail(total, state, w_update1, w_update2, 0)
    state_out[...] = new_state
    projected1 = dot(new_state, w_in[1]).astype(bf16)
    proj_out[...] = projected1
    proj_table[...] = projected1.astype(f32)
    pick_send_rows(proj_table, send, send_out)


def filter_kernel(chord, w1, w2, out, wide1, wide2):
    step = pl.program_id(0)

    @pl.when(step == 0)
    def _():
        fill_filter_weights(w1, w2, 1, wide1, wide2)

    def make(i, carry):
        make_filters(chord, step * 2 + i, wide1, wide2, out.at[i])
        return carry

    lax.fori_loop(0, 2, make, 0)


def last_layer_kernel(
    slots_s, core, filters, x_low, x_own, x_high, projected, state,
    w_update1, w_update2, w_charge, phase, axis, digits,
    state_out, keep_out, give_out,
    table, total, left, sums,
):
    step = pl.program_id(0)

    @pl.when(step == 0)
    def _():
        fill_table(table, projected, (x_low, x_own, x_high), H)
        total[...] = jnp.zeros_like(total)

    def use(i, carry):
        add_messages(table, slots_s, filters.at[i // 4], total, i % 4, step * 2 + i // 4)
        return carry

    lax.fori_loop(0, 8, use, 0)

    @pl.when(step == 3)
    def _():
        new_state = update_tail(total, state, w_update1, w_update2, 1)
        state_out[...] = new_state
        charges = dot(w_charge[...], new_state, ((1,), (1,))).astype(bf16).astype(f32)
        for n in range(KX):
            left[n * Q : (n + 1) * Q, :T] = (charges * axis[n : n + 1, :]).astype(bf16)
            left[n * Q : (n + 1) * Q, T:] = (charges * axis[8 + n : 9 + n, :]).astype(bf16)
        sums[...] = jnp.zeros_like(sums)
        sums[:ROWS, : 2 * BETA] = dot(left[...], phase[...], ((1,), (1,)))
        sums[ROWS:, :] = digits[...]
        mine = pl.multiple_of(core[0] * HALF, HALF)
        keep_out[...] = sums[pl.ds(mine, HALF), :].astype(bf16)
        give_out[...] = sums[pl.ds(pl.multiple_of(HALF - mine, HALF), HALF), :].astype(bf16)


def field_kernel(
    core, own_half, other_half, phase, axis, screening, head, w_potential, w_energy,
    potentials_out, energies_out, response, sums,
):
    mine = pl.multiple_of(core[0] * HALF, HALF)
    sums[pl.ds(mine, HALF), :] = own_half[...].astype(f32)
    sums[pl.ds(pl.multiple_of(HALF - mine, HALF), HALF), :] = other_half[...].astype(f32)
    lane = rows_of((1, SUM_LANES), 1)
    beta = jnp.where(lane >= BETA, lane - BETA, lane)
    y = (beta * 79) >> 10
    ky = y - 6
    kz = beta - y * YZ - 6
    plane_sq = (ky * ky + kz * kz).astype(f32)
    digits = sums[ROWS:, :]
    packed = digits[0:8] + 3.0 * digits[8:16]
    ahead = pltpu.roll(packed, SUM_LANES - BETA, 1)
    behind = pltpu.roll(packed, BETA, 1)
    lane8 = rows_of((8, SUM_LANES), 1)
    count = jnp.where(lane8 < BETA, packed + 9.0 * ahead, behind + 9.0 * packed)
    square = rows_of((Q, Q), 0) == rows_of((Q, Q), 1)
    screen = jnp.sum(jnp.where(square, jnp.broadcast_to(screening[...], (Q, Q)), 0.0), axis=1, keepdims=True)
    for n in range(KX):
        norm_sq = plane_sq + float(n * n)
        kernel = jnp.exp(norm_sq * (-1.0 / 64.0)) * count[n : n + 1, :] / (norm_sq + screen)
        value = kernel * sums[n * Q : (n + 1) * Q, :]
        response[n * Q : (n + 1) * Q, :] = value[:, : 2 * BETA].astype(bf16)
    field = dot(response[...], phase[...])
    total = jnp.zeros((Q, T), f32)
    for n in range(KX):
        part = field[n * Q : (n + 1) * Q]
        total = total + part[:, :T] * axis[n : n + 1, :] + part[:, T:] * axis[8 + n : 9 + n, :]
    potentials = total * (4.0 / 256.0)
    potentials_out[...] = potentials
    summed = head[...] + dot(potentials.astype(bf16), w_potential[...], ((0,), (0,)))
    readout = silu(summed).astype(bf16)
    energies_out[...] = dot(w_energy[...], readout, ((1,), (1,)))


VMEM = pl.BlockSpec(memory_space=pltpu.VMEM)
SMEM = pl.BlockSpec(memory_space=pltpu.SMEM)


def shape(*dims, dtype=f32):
    return jax.ShapeDtypeStruct(dims, dtype)


def call(kernel, ins, outs, scratch, flops, moved):
    return pl.pallas_call(
        kernel,
        out_shape=outs,
        in_specs=ins,
        out_specs=jax.tree.map(lambda _: VMEM, outs),
        scratch_shapes=scratch,
        cost_estimate=pl.CostEstimate(flops=flops, bytes_accessed=moved, transcendentals=0),
    )


def near(x):
    return pltpu.with_memory_space_constraint(x, pltpu.VMEM)


def halo(block):
    for axis in ("gx", "yz"):
        count = lax.axis_size(axis)
        forward = [(i, (i + 1) % count) for i in range(count)]
        backward = [(target, source) for source, target in forward]
        low = lax.ppermute(block, axis, forward)
        high = lax.ppermute(block, axis, backward)
        if axis == "gx":
            block = jnp.concatenate([low, block, high], axis=0)
    return near(low), near(block), near(high)


RINGS = ((4, 8, 12), (32, 64, 96), (2, 16, 18))


def exchange(part, offset):
    count = lax.axis_size("gx") * lax.axis_size("yz")
    return lax.ppermute(part, ("gx", "yz"), [(i, i ^ offset) for i in range(count)])


def sum_everywhere(keep, give):
    part = (keep.astype(f32) + exchange(give, 1).astype(f32)).astype(bf16)
    for offsets in RINGS:
        taken = [exchange(part, o) for o in offsets]
        total = part.astype(f32)
        for one in taken:
            total = total + one.astype(f32)
        part = total.astype(bf16)
    return part, exchange(part, 1)


def shards(
    features, frac, neighbours, nbr_mask, send_list, wavevectors, w_in, w_filter1, w_filter2,
    w_update1, w_update2, w_charge, screening, w_head, w_potential, w_energy,
):
    projected, sent = call(
        first_kernel, [SMEM, VMEM, VMEM, VMEM, VMEM],
        (shape(T, C, dtype=bf16), shape(PACK, C, dtype=bf16)),
        [pltpu.VMEM((T, C), f32), pltpu.VMEM((32, 128), f32)], 20_000_000, 300_000,
    )(send_list, send_list.reshape(2, 128), features, frac, w_in)
    slots, phase, axis, digits = call(
        prepare_kernel, [VMEM] * 4,
        (shape(4 * K, 128, dtype=i32), shape(2 * BETA, 2 * T, dtype=bf16), shape(16, T), shape(16, SUM_LANES)),
        [pltpu.VMEM((2, BETA, T), f32)], 2_000_000_000, 4_000_000,
    )(neighbours, nbr_mask, frac, wavevectors)
    x_low, x_own, x_high = halo(sent)
    state, projected, sent, chord = call(
        layer_kernel, [pl.BlockSpec(memory_space=pl.ANY), SMEM] + [VMEM] * 12,
        (shape(T, C, dtype=bf16), shape(T, C, dtype=bf16), shape(H, C, dtype=bf16), shape(4 * K, 128)),
        [
            pltpu.VMEM((SLOTS + 8, C), f32), pltpu.VMEM((72, 128), f32),
            pltpu.VMEM((4 * NR, 4 * C), bf16), pltpu.VMEM((2 * C, 2 * C), bf16),
            pltpu.VMEM((8, 2, T, 2 * C), bf16),
            pltpu.VMEM((T, C), f32), pltpu.VMEM((T, C), f32),
            pltpu.SMEM((K * T,), i32), pltpu.SemaphoreType.DMA,
        ], 4_000_000_000, 4_000_000,
    )(
        slots.reshape(-1), send_list, slots, near(frac), x_low, x_own, x_high, near(projected), near(features),
        near(w_filter1), near(w_filter2), near(w_update1), near(w_update2), near(w_in),
    )
    x_low, x_own, x_high = halo(sent)
    whole = lambda a: pl.BlockSpec(a.shape, lambda i: (0,) * a.ndim)
    block = pl.BlockSpec((2, 2, T, 2 * C), lambda i: (i, 0, 0, 0))
    filters = pl.pallas_call(
        filter_kernel, grid=(4,),
        out_shape=shape(8, 2, T, 2 * C, dtype=bf16),
        in_specs=[whole(chord), whole(w_filter1), whole(w_filter2)], out_specs=block,
        scratch_shapes=[pltpu.VMEM((4 * NR, 4 * C), bf16), pltpu.VMEM((2 * C, 2 * C), bf16)],
        cost_estimate=pl.CostEstimate(flops=4_000_000_000, bytes_accessed=8_000_000, transcendentals=0),
    )(chord, w_filter1, w_filter2)
    phase, axis = near(phase), near(axis)
    rest = (x_low, x_own, x_high, near(projected), near(state), near(w_update1), near(w_update2))
    rest = rest + (near(w_charge.T), phase, axis, near(digits))
    half = shape(HALF, SUM_LANES, dtype=bf16)
    half_spec = pl.BlockSpec(half.shape, lambda i: (0, 0))
    core = (lax.axis_index("yz") & 1).reshape(1)
    embeddings, keep, give = pl.pallas_call(
        last_layer_kernel, grid=(4,),
        out_shape=(shape(T, C, dtype=bf16), half, half),
        in_specs=[SMEM, SMEM, block] + [whole(a) for a in rest],
        out_specs=(pl.BlockSpec((T, C), lambda i: (0, 0)), half_spec, half_spec),
        scratch_shapes=[
            pltpu.VMEM((SLOTS + 8, C), f32), pltpu.VMEM((T, C), f32), pltpu.VMEM((ROWS, 2 * T), bf16),
            pltpu.VMEM((SUM_ROWS, SUM_LANES), f32),
        ],
        cost_estimate=pl.CostEstimate(flops=1_000_000_000, bytes_accessed=8_000_000, transcendentals=0),
    )(slots.reshape(-1), core, filters, *rest)
    own_half, other_half = sum_everywhere(keep, give)
    head = dot(embeddings, w_head)
    potentials, energies = call(
        field_kernel, [SMEM] + [VMEM] * 8, (shape(Q, T), shape(1, T)),
        [pltpu.VMEM((ROWS, 2 * BETA), bf16), pltpu.VMEM((SUM_ROWS, SUM_LANES), f32)], 100_000_000, 2_000_000,
    )(
        core, near(own_half), near(other_half), phase, axis, near(screening.reshape(1, Q)), near(head),
        near(w_potential), near(w_energy.reshape(1, C)),
    )
    return embeddings, potentials, energies.reshape(T)


def solution(mesh):
    atoms = ("gx", "yz")
    return jax.shard_map(
        shards,
        mesh=mesh,
        in_specs=(P(atoms, None), P(None, atoms), P(None, atoms), P(None, atoms), P(atoms), P(None, atoms))
        + (P(),) * 10,
        out_specs=(P(atoms, None), P(None, atoms), P(atoms)),
        check_vma=False,
    )
```
